512 devices in a mesh: row: 32 (over x, z_hi, core), col: 16 (over y, z_lo).
Axes of the slice: x: 4, y: 8, z: 8 (z_hi: 4, z_lo: 2; z = z_hi * 2 + z_lo), core: 2. Of those that a mesh axis runs over, the one named last changes fastest.
Arguments:
- hidden_input: bfloat16 [4096, 2048], P('row', 'col'), may hold values from -6 to 6
- norm_gain: float32 [2048], P('col'), may hold values from 0.5 to 1.5
- router_weight: bfloat16 [2048, 4], P('col'), may hold values from -0.25 to 0.25
- expert_in: bfloat16 [4, 2, 2048, 4096], P(None, None, 'row', 'col'), may hold values from -0.125 to 0.125
- expert_out: bfloat16 [4, 4096, 2048], P(None, 'col', 'row'), may hold values from -0.09375 to 0.09375
- adapter_down: bfloat16 [16, 2048, 16], P(None, 'col'), may hold values from -0.125 to 0.125
- adapter_up: bfloat16 [16, 16, 2048], P(None, None, 'col'), may hold values from -0.375 to 0.375
- routes: int32 [4096, 2], P('row'), may hold values from 0 to 3, all different within a row
- lengths: int32 [16], replicated, may hold values from 1 to 1024, 4096 in all
- adapter_ids: int32 [16], replicated, may hold values from 0 to 15
Outputs:
- layer_out: bfloat16 [4096, 2048], P('row', 'col')
The draws below stay inside these ranges and needn't reach their ends.
Inputs may be any that keep to these rules, and one draw needn't show every extreme that they name: `routes`: each token names two different experts. The lengths sum to 4096.
All inputs are finite; a program needn't handle non-finite values.
Results may differ from the reference program's by a relative error of at most 0.0059.
Values may be sent and summed in bfloat16 or wider, within the bound.
A program may use at most 64 MiB of HBM per device.

```python
import math
import jax
import jax.numpy as jnp
import numpy as np
from jax import lax

D = 2048
FF = 4096
EXPERTS = 4
RANK = 16
ADAPTERS = 16
REQUESTS = 16
TOKENS = 4096
LONGEST = 1024


def with_ends(entries, own_key, smallest, top_value):
    index_at = [jax.random.randint(jax.random.fold_in(own_key, axis), (), 0, length) for axis, length in enumerate(entries.shape)]
    longest = entries.shape.index(max(entries.shape))
    neighbour = index_at[:longest] + [(index_at[longest] + 1) % entries.shape[longest]] + index_at[longest + 1:]
    return entries.at[tuple(index_at)].set(smallest).at[tuple(neighbour)].set(top_value)


def block_levels(stream_key, extent, shards, low, high):
    gain, own = 1.0, jax.random.fold_in(stream_key, 6)
    for axis_at, shards_of in shards:
        heights = jnp.exp(jax.random.uniform(jax.random.fold_in(own, axis_at), (shards_of,), jnp.float32, low / len(shards), high / len(shards)))
        gain = gain * jnp.repeat(heights, extent[axis_at] // shards_of).reshape([-1 if axis == axis_at else 1 for axis in range(len(extent))])
    return gain


def distinct(rng, rows, number_of, top, lift):
    sequence = jax.random.permutation(jax.random.fold_in(rng, 1), number_of)
    favour = sequence
    for power in range(3):
        favour = favour * favour // number_of
    favour = favour * lift // number_of
    lots = jax.random.randint(jax.random.fold_in(rng, 2), (rows, number_of), 0, 4096) + favour
    fixed_rows = jax.random.permutation(jax.random.fold_in(rng, 3), rows)[jnp.arange(number_of) % rows]
    lots = jnp.where(jnp.arange(rows)[:, None] == fixed_rows[None, :], 1 << 14, lots)
    score = lots * number_of + jnp.arange(number_of)
    return lax.top_k(score.astype(jnp.int32), top)[1].astype(jnp.int32)


def split_up(count, total, reach, slope):
    loads = [(1 << 20) // math.isqrt(grade ** slope) + 1 for grade in range(2, count + 1)]
    spare, holding = total - reach - (count - 1), [1] * (count - 1)
    while spare > 0:
        free = [i for i in range(count - 1) if holding[i] < reach]
        mass, remaining = sum([loads[i] for i in free]), spare
        for i in free:
            addition = min(reach - holding[i], max(1, remaining * loads[i] // mass), spare)
            holding[i] = holding[i] + addition
            spare = spare - addition
    return np.array([reach] + holding)


def ragged_sizes(stream_key, number_of, total, limit, skew):
    if number_of == 2:
        one = jax.random.randint(stream_key, (), max(1, total - limit), min(limit, total - 1) + 1)
        return jnp.stack([one, total - one])
    sizes = jnp.asarray(split_up(number_of, total, limit, skew), jnp.int32)
    twos = (number_of - 1) // 2
    source_of, taker = sizes[1:1 + 2 * twos:2], sizes[2:2 + 2 * twos:2]
    margin = jnp.minimum(source_of - 1, limit - taker)
    moved = jax.random.randint(jax.random.fold_in(stream_key, 1), (twos,), 0, 1 << 20) % (margin + 1)
    sizes = sizes.at[1:1 + 2 * twos:2].set(source_of - moved).at[2:2 + 2 * twos:2].set(taker + moved)
    return sizes[jax.random.permutation(jax.random.fold_in(stream_key, 2), number_of)]


def scatter_about(own_key, shape, scale, reach, pieces=(), kind=jnp.bfloat16):
    result = scale * jax.random.normal(own_key, shape, jnp.float32)
    if pieces:
        result = result * block_levels(own_key, shape, pieces, -0.22, 0.18)
    return jnp.clip(result, -reach, reach).astype(kind)


def setup_inputs(seed: int = 0) -> dict:
    key_list = jax.random.split(jax.random.key(seed), 11)
    hidden_input = scatter_about(key_list[0], (TOKENS, D), 1.0, 6.0, ((0, 32), (1, 16)))
    norm_gain = jnp.clip(1.0 + 0.1 * jax.random.normal(key_list[1], (D,), jnp.float32), 0.5, 1.5)
    router_weight = scatter_about(key_list[2], (D, EXPERTS), (D // 4) ** -0.5, 0.25, ((0, 16),))
    expert_in = scatter_about(key_list[3], (EXPERTS, 2, D, FF), D ** -0.5, 0.125, ((2, 32), (3, 16)))
    expert_out = scatter_about(key_list[4], (EXPERTS, FF, D), FF ** -0.5, 0.09375, ((1, 16), (2, 32)))
    adapter_down = scatter_about(key_list[5], (ADAPTERS, D, RANK), D ** -0.5, 0.125, ((1, 16),))
    adapter_up = scatter_about(key_list[6], (ADAPTERS, RANK, D), (RANK * 16) ** -0.5, 0.375, ((2, 16),))
    routes = distinct(key_list[7], TOKENS, EXPERTS, 2, 8192)
    lengths = ragged_sizes(key_list[8], REQUESTS, TOKENS, LONGEST, 2).astype(jnp.int32)
    adapter_ids = with_ends(jax.random.randint(key_list[9], (REQUESTS,), 0, ADAPTERS), jax.random.fold_in(key_list[9], 1), 0, ADAPTERS - 1).astype(jnp.int32)
    return {"hidden_input": hidden_input, "norm_gain": norm_gain, "router_weight": router_weight, "expert_in": expert_in, "expert_out": expert_out, "adapter_down": adapter_down, "adapter_up": adapter_up, "routes": routes, "lengths": lengths, "adapter_ids": adapter_ids}


epsilon = 1e-05
adapter_scaling_factor = 2.0

def reference(hidden_input, norm_gain, router_weight, expert_in, expert_out, adapter_down, adapter_up, routes, lengths, adapter_ids):
    stream = hidden_input.astype(jnp.float32)
    inverse = lax.rsqrt(lax.optimization_barrier(jnp.mean(stream * stream, axis=1)) + epsilon)
    normed = stream * inverse[:, None] * norm_gain
    rounded = normed.astype(jnp.bfloat16)
    logits = jnp.dot(normed, router_weight.astype(jnp.float32), precision=lax.Precision.HIGHEST)
    chosen = jnp.take_along_axis(logits, routes, axis=1)
    first_gate = jax.nn.sigmoid(chosen[:, 0] - chosen[:, 1])
    second_gate = jax.nn.sigmoid(chosen[:, 1] - chosen[:, 0])
    bounds = jnp.cumsum(lengths).astype(jnp.int32)
    position = jnp.arange(TOKENS, dtype=jnp.int32)
    request = lax.optimization_barrier(jnp.sum((position[:, None] >= bounds[None, :]).astype(jnp.int32), axis=1))
    adapter = jnp.take(adapter_ids, request)
    selector = (adapter[:, None] == jnp.arange(ADAPTERS, dtype=jnp.int32)[None, :]).astype(jnp.float32)
    down_flat = jnp.transpose(adapter_down.astype(jnp.float32), (1, 0, 2)).reshape(D, ADAPTERS * RANK)
    projected = jnp.dot(normed, down_flat, precision=lax.Precision.HIGHEST).reshape(TOKENS, ADAPTERS, RANK)
    latent = lax.optimization_barrier(jnp.sum(projected * selector[:, :, None], axis=1))
    spread = (selector[:, :, None] * latent[:, None, :]).reshape(TOKENS, ADAPTERS * RANK)
    up_matrix = adapter_up.astype(jnp.float32).reshape(ADAPTERS * RANK, D)
    adapter_delta = jnp.dot(spread, up_matrix, precision=lax.Precision.HIGHEST)
    mixture = jnp.zeros((TOKENS, D), jnp.float32)
    for expert in range(EXPERTS):
        gate_value = jnp.dot(rounded, expert_in[expert, 0], preferred_element_type=jnp.float32)
        upward = jnp.dot(rounded, expert_in[expert, 1], preferred_element_type=jnp.float32)
        hidden_state = (jax.nn.silu(gate_value) * upward).astype(jnp.bfloat16)
        output = jnp.dot(hidden_state, expert_out[expert], preferred_element_type=jnp.float32)
        weight = jnp.where(routes[:, 0] == expert, first_gate, jnp.float32(0.0)) + jnp.where(routes[:, 1] == expert, second_gate, jnp.float32(0.0))
        mixture = mixture + output * weight[:, None]
    return (mixture + adapter_scaling_factor * adapter_delta).astype(jnp.bfloat16)
```

```python
import jax
import jax.numpy as jnp
from jax import lax
from jax.experimental import pallas as pl
from jax.experimental.pallas import tpu as pltpu
from jax.sharding import PartitionSpec as P

NX, NZ, NC = 4, 4, 16
RING = 8
B = 128
D = 2048
F = 256
SLAB = 64
RANK, ADAPTERS, REQUESTS = 16, 16, 16
epsilon = 1e-05
adapter_scaling_factor = 2.0

MESH = pl.DeviceIdType.MESH
F32, BF16 = jnp.float32, jnp.bfloat16
HIGH = lax.Precision.HIGHEST
NT = (((1,), (1,)), ((), ()))
TN = (((0,), (0,)), ((), ()))


def kernel(
    lengths, adapter_ids, h_ref, gain_ref, small_ref, up_ref, routes_ref, win_ref, wout_ref, out_ref,
    xb, nb, wb, ob, hid, pr, lr, tr, inv_b, gate_b, pstage, lstage,
    rs_send, rs_recv, sm_send, sm_recv,
    local_sem, az_s, az_r, ab_s, ab_r, wz_s, wz_r, wx_s, wx_r, wp_s, wp_r,
    p_s, p_r, l_s, l_r, t_s, t_r, rs_s, rs_r, sm_s, sm_r,
):
    row, col = lax.axis_index("row"), lax.axis_index("col")
    k = lax.rem(row, 2)
    chip_row = lax.div(row, 2)
    x, zh = lax.div(chip_row, NZ), lax.rem(chip_row, NZ)
    y, zl = lax.div(col, 2), lax.rem(col, 2)
    z = zh * 2 + zl
    big, small = y * (1 - k) + z * k, z * (1 - k) + y * k
    sy, sz = RING * (1 - k) + k, RING * k + (1 - k)

    def at_plane(b, s):
        yy, zz = b * (1 - k) + s * k, s * (1 - k) + b * k
        return ((x * NZ + lax.div(zz, 2)) * 2 + k, yy * 2 + lax.rem(zz, 2))

    def at_x(xx):
        return ((lax.rem(xx + NX, NX) * NZ + zh) * 2 + k, col)

    def ring(v):
        return lax.rem(v + RING, RING)

    pending = []

    def send(src, dst, s_sem, r_sem, device):
        copy = pltpu.make_async_remote_copy(
            src_ref=src, dst_ref=dst, send_sem=s_sem, recv_sem=r_sem, device_id=device, device_id_type=MESH
        )
        copy.start()
        pending.append(copy)

    partner = (chip_row * 2 + 1 - k, col)

    def arrived(dst, s_sem, r_sem):
        pltpu.make_async_remote_copy(
            src_ref=dst, dst_ref=dst, send_sem=s_sem, recv_sem=r_sem, device_id=partner, device_id_type=MESH
        ).wait_recv()

    peers = [(row, lax.rem(col + d, NC)) for d in range(1, NC)]
    for d in range(1, NZ):
        for e in range(2):
            peers.append(((x * NZ + lax.rem(zh + d, NZ)) * 2 + k, y * 2 + e))
    peers += [at_x(x + 1), at_x(x - 1), partner]
    barrier = pltpu.get_barrier_semaphore()
    for peer in peers:
        pl.semaphore_signal(barrier, inc=1, device_id=peer, device_id_type=MESH)
    pl.semaphore_wait(barrier, len(peers))

    mine = xb.at[big * RING + small]
    own_x = pltpu.make_async_copy(h_ref, mine, local_sem.at[0])
    own_x.start()
    for d in range(1, RING):
        send(h_ref, mine, az_s.at[d], az_r.at[d], at_plane(big, ring(small + d)))

    def rows_of(xx, jj):
        zz = lax.rem(zh - jj + NZ, NZ)
        r = (lax.rem(xx + NX, NX) * NZ + zz) * 2 + k
        return pl.ds(pl.multiple_of(r * SLAB, SLAB), SLAB)

    my_rows = rows_of(x, 0)
    own_w = [
        pltpu.make_async_copy(win_ref.at[zh], wb.at[pl.ds(0, 2), my_rows], local_sem.at[1]),
        pltpu.make_async_copy(wout_ref.at[zh], wb.at[2, my_rows], local_sem.at[2]),
    ]
    for copy in own_w:
        copy.start()
    for j in (2, 1, 3):
        e = lax.rem(zh + j, NZ)
        to = ((x * NZ + e) * 2 + k, col)
        send(win_ref.at[e], wb.at[pl.ds(0, 2), my_rows], wz_s.at[j, 0], wz_r.at[j, 0], to)
        send(wout_ref.at[e], wb.at[2, my_rows], wz_s.at[j, 1], wz_r.at[j, 1], to)

    def w_piece(xx, j):
        return wb.at[:, rows_of(xx, j)]

    def w_out(xx, j, slot, right=False, left=False):
        piece = w_piece(xx, j)
        if right:
            m = j if slot == 0 else 4 + j
            send(piece, piece, wx_s.at[0, m], wx_r.at[0, m], at_x(x + 1))
        if left:
            m = j if slot == 0 else 4 + j
            send(piece, piece, wx_s.at[1, m], wx_r.at[1, m], at_x(x - 1))
        send(piece, piece, wp_s.at[slot * 4 + j], wp_r.at[slot * 4 + j], partner)

    def w_own(j):
        if j == 0:
            for copy in own_w:
                copy.wait()
        else:
            rows = rows_of(x, j)
            arrived(wb.at[pl.ds(0, 2), rows], wz_s.at[j, 0], wz_r.at[j, 0])
            arrived(wb.at[2, rows], wz_s.at[j, 1], wz_r.at[j, 1])
        w_out(x, j, 0, right=True, left=True)

    def w_near(j):
        arrived(w_piece(x - 1, j), wx_s.at[0, j], wx_r.at[0, j])
        w_out(x - 1, j, 1, right=j < 2)
        arrived(w_piece(x + 1, j), wx_s.at[1, j], wx_r.at[1, j])
        w_out(x + 1, j, 2, left=j >= 2)

    def w_far(j):
        side = 0 if j < 2 else 1
        arrived(w_piece(x + 2, j), wx_s.at[side, 4 + j], wx_r.at[side, 4 + j])
        w_out(x + 2, j, 3)

    w_own(0)

    hx = h_ref[...].astype(F32)
    ones = jnp.ones((8, B), F32)
    squares = lax.dot_general(ones, hx * hx, NT, precision=HIGH, preferred_element_type=F32)
    projected = lax.dot_general(small_ref[...], hx, NT, precision=HIGH, preferred_element_type=F32)
    line = lax.broadcasted_iota(jnp.int32, (8, B), 0)
    tile = projected[ADAPTERS * RANK :]
    tile = jnp.where(line == 0, squares, tile)
    tile = jnp.where(line == 5, jnp.broadcast_to(gain_ref[...], (8, B)), tile)
    pstage[...] = tile
    position = row * B + lax.broadcasted_iota(jnp.int32, (1, B), 1)
    bound = lengths[0]
    request = (position >= bound).astype(jnp.int32)
    for i in range(1, REQUESTS):
        bound = bound + lengths[i]
        request = request + (position >= bound).astype(jnp.int32)
    adapter = jnp.zeros((1, B), jnp.int32)
    for i in range(REQUESTS):
        adapter = jnp.where(request == i, adapter_ids[i], adapter)
    adapter = jnp.broadcast_to(adapter, (RANK, B))
    part = jnp.zeros((RANK, B), F32)
    for a in range(ADAPTERS):
        part = part + jnp.where(adapter == a, projected[a * RANK : (a + 1) * RANK], 0.0)
    lstage[...] = part
    pr[col] = tile
    lr[col] = part
    for d in range(1, NC):
        send(pstage, pr.at[col], p_s.at[d], p_r.at[d], (row, lax.rem(col + d, NC)))

    def a_piece(b, p):
        return xb.at[pl.ds(ring(b) * RING + 4 * p, 4)]

    def a_send(step, p, way):
        b = big - (step - 1) if way == 0 else big + (step - 1)
        to = at_plane(ring(big + 1), small) if way == 0 else at_plane(ring(big - 1), small)
        m = (step - 1) * 2 + p
        send(a_piece(b, p), a_piece(b, p), ab_s.at[way, m], ab_r.at[way, m], to)

    def a_step(step):
        for p in range(2):
            for way in range(2):
                if step == 4 and p != way:
                    continue
                m = (step - 1) * 2 + p
                b = big - step if way == 0 else big + step
                arrived(a_piece(b, p), ab_s.at[way, m], ab_r.at[way, m])
                if step < 3 or (step == 3 and p == way):
                    a_send(step + 1, p, way)

    own_x.wait()
    for d in range(1, RING):
        arrived(xb.at[big * RING + ring(small - d)], az_s.at[d], az_r.at[d])
    for p in range(2):
        a_send(1, p, 0)
        a_send(1, p, 1)

    w_own(1)
    w_own(3)
    w_near(0)

    for d in range(1, NC):
        arrived(pr.at[lax.rem(col - d + NC, NC)], p_s.at[d], p_r.at[d])
    total = pr[0]
    for i in range(1, NC):
        total = total + pr[i]
    inverse = lax.rsqrt(total[0:1] / D + epsilon)
    logits = [total[1 + e : 2 + e] * inverse for e in range(NZ)]
    route = [routes_ref[0:1, :], routes_ref[1:2, :]]
    chosen = []
    for i in range(2):
        value = jnp.zeros((1, B), F32)
        for e in range(NZ):
            value = jnp.where(route[i] == e, logits[e], value)
        chosen.append(value)
    gates = [jax.nn.sigmoid(chosen[0] - chosen[1]), jax.nn.sigmoid(chosen[1] - chosen[0])]
    share = jnp.where(line == 0, jnp.broadcast_to(inverse, (8, B)), 0.0)
    for e in range(NZ):
        weight = jnp.where(route[0] == e, gates[0], 0.0) + jnp.where(route[1] == e, gates[1], 0.0)
        share = jnp.where(line == 1 + e, jnp.broadcast_to(weight, (8, B)), share)
    tr[zh] = share
    for d in range(1, NZ):
        to = ((x * NZ + lax.rem(zh + d, NZ)) * 2 + k, col)
        send(tr.at[zh], tr.at[zh], t_s.at[d], t_r.at[d], to)
    for d in range(1, NC):
        send(lstage, lr.at[col], l_s.at[d], l_r.at[d], (row, lax.rem(col + d, NC)))

    a_step(1)
    w_own(2)
    w_near(1)
    a_step(2)
    w_near(3)
    w_near(2)
    w_far(0)
    a_step(3)

    for d in range(1, NZ):
        arrived(tr.at[lax.rem(zh - d + NZ, NZ)], t_s.at[d], t_r.at[d])
    for i in range(NZ):
        rows = tr[i]
        gate_row = tr[i, pl.ds(1 + zh, 1), :]
        both = jnp.where(line == 0, rows, jnp.broadcast_to(gate_row, (8, B)))
        turned = jnp.transpose(both)
        inv_b[i] = jnp.broadcast_to(turned[:, 0:1], (B, B))
        gate_b[i] = jnp.broadcast_to(turned[:, 1:2], (B, B))

    def normalise(b):
        @pl.loop(0, RING)
        def _(s):
            yy, zz = b * (1 - k) + s * k, s * (1 - k) + b * k
            c, t = yy * 2 + lax.rem(zz, 2), lax.div(zz, 2)
            value = xb[b * RING + s].astype(F32) * inv_b[t] * pr[c, pl.ds(5, 1), :]
            nb[pl.ds(pl.multiple_of(t * B, B), B), pl.ds(pl.multiple_of(c * B, B), B)] = value.astype(BF16)

    w_far(1)
    normalise(big)
    for d in range(1, 4):
        normalise(ring(big - d))
        normalise(ring(big + d))
    w_far(3)
    w_far(2)
    a_step(4)
    normalise(ring(big + 4))
    for slot in range(4):
        xx = (x, x - 1, x + 1, x + 2)[slot]
        for j in range(4):
            zz = lax.rem(zh - j + NZ, NZ)
            r = (lax.rem(xx + NX, NX) * NZ + zz) * 2 + 1 - k
            arrived(
                wb.at[:, pl.ds(pl.multiple_of(r * SLAB, SLAB), SLAB)], wp_s.at[slot * 4 + j], wp_r.at[slot * 4 + j]
            )

    @pl.loop(0, 2)
    def _(i):
        rows = pl.ds(pl.multiple_of(i * 256, 256), 256)
        tokens = nb[rows, :]
        gate = jnp.dot(tokens, wb[0], preferred_element_type=F32)
        up = jnp.dot(tokens, wb[1], preferred_element_type=F32)
        hid[rows, :] = (jax.nn.silu(gate) * up).astype(BF16)

    @pl.loop(0, RING)
    def _(yy):
        weights = wb[2, pl.ds(pl.multiple_of(yy * 256, 256), 256), :]
        result = lax.dot_general(hid[...], weights, NT, preferred_element_type=F32)
        for t in range(NZ):
            for half in range(2):
                block = result[t * B : (t + 1) * B, half * B : (half + 1) * B]
                ob[yy * sy + (t * 2 + half) * sz] = block * gate_b[t]

    def r_send(j, p, way):
        m = (4 - j) * 2 + p
        b = ring(big + j) if way == 0 else ring(big - j)
        own = ob[pl.ds(b * RING + 4 * p, 4)]
        if j == 3 and p == way or j < 3:
            before = m - 2
            arrived(rs_recv.at[way, before], rs_s.at[way, before], rs_r.at[way, before])
            own = own + rs_recv[way, before].astype(F32)
        rs_send[way, m] = own.astype(BF16)
        to = at_plane(ring(big + 1), small) if way == 0 else at_plane(ring(big - 1), small)
        send(rs_send.at[way, m], rs_recv.at[way, m], rs_s.at[way, m], rs_r.at[way, m], to)

    r_send(4, 0, 0)
    r_send(4, 1, 1)
    r_send(3, 1, 0)
    r_send(3, 0, 1)
    r_send(3, 0, 0)
    r_send(3, 1, 1)
    for j in (2, 1):
        r_send(j, 1, 0)
        r_send(j, 0, 1)
        r_send(j, 0, 0)
        r_send(j, 1, 1)

    for d in range(1, NC):
        arrived(lr.at[lax.rem(col - d + NC, NC)], l_s.at[d], l_r.at[d])
    latent = lr[0]
    for i in range(1, NC):
        latent = latent + lr[i]
    latent = latent * jnp.broadcast_to(inverse, (RANK, B))
    spread = jnp.concatenate([jnp.where(adapter == a, latent, 0.0) for a in range(ADAPTERS)], axis=0)
    delta = lax.dot_general(spread, up_ref[...].astype(F32), TN, precision=HIGH, preferred_element_type=F32)

    for p in range(2):
        total4 = ob[pl.ds(big * RING + 4 * p, 4)]
        for way in range(2):
            m = 6 + p
            arrived(rs_recv.at[way, m], rs_s.at[way, m], rs_r.at[way, m])
            total4 = total4 + rs_recv[way, m].astype(F32)
        ob[pl.ds(big * RING + 4 * p, 4)] = total4
        sm_send[pl.ds(4 * p, 4)] = total4.astype(BF16)
    for d in range(1, RING):
        s = ring(small + d)
        send(sm_send.at[s], sm_recv.at[small], sm_s.at[d], sm_r.at[d], at_plane(big, s))
    result = ob[big * RING + small] + adapter_scaling_factor * delta
    for d in range(1, RING):
        s = ring(small - d)
        arrived(sm_recv.at[s], sm_s.at[d], sm_r.at[d])
        result = result + sm_recv[s].astype(F32)
    out_ref[...] = result.astype(BF16)
    for copy in pending:
        copy.wait_send()


def on_device(
    hidden_input, norm_gain, router_weight, expert_in, expert_out, adapter_down, adapter_up, routes, lengths, adapter_ids
):
    down = jnp.transpose(adapter_down, (0, 2, 1)).reshape(ADAPTERS * RANK, B)
    pad = jnp.zeros((1, B), BF16)
    table = jnp.concatenate([down, pad, router_weight.T, pad, pad, pad], axis=0).astype(F32) * norm_gain[None, :]
    vmem = pl.BlockSpec(memory_space=pltpu.VMEM)
    smem = pl.BlockSpec(memory_space=pltpu.SMEM)
    hbm = pl.BlockSpec(memory_space=pl.ANY)
    dma = pltpu.SemaphoreType.DMA
    return pl.pallas_call(
        kernel,
        out_shape=jax.ShapeDtypeStruct((B, B), BF16),
        in_specs=[smem, smem, vmem, vmem, vmem, vmem, vmem, hbm, hbm],
        out_specs=vmem,
        scratch_shapes=[
            pltpu.VMEM((RING * RING, B, B), BF16),
            pltpu.VMEM((NZ * B, D), BF16),
            pltpu.VMEM((3, D, F), BF16),
            pltpu.VMEM((RING * RING, B, B), F32),
            pltpu.VMEM((NZ * B, F), BF16),
            pltpu.VMEM((NC, 8, B), F32),
            pltpu.VMEM((NC, RANK, B), F32),
            pltpu.VMEM((NZ, 8, B), F32),
            pltpu.VMEM((NZ, B, B), F32),
            pltpu.VMEM((NZ, B, B), F32),
            pltpu.VMEM((8, B), F32),
            pltpu.VMEM((RANK, B), F32),
            pltpu.VMEM((2, 8, 4, B, B), BF16),
            pltpu.VMEM((2, 8, 4, B, B), BF16),
            pltpu.VMEM((RING, B, B), BF16),
            pltpu.VMEM((RING, B, B), BF16),
            dma((3,)),
            dma((RING,)), dma((RING,)),
            dma((2, 8)), dma((2, 8)),
            dma((NZ, 2)), dma((NZ, 2)),
            dma((2, 8)), dma((2, 8)),
            dma((16,)), dma((16,)),
            dma((NC,)), dma((NC,)),
            dma((NC,)), dma((NC,)),
            dma((NZ,)), dma((NZ,)),
            dma((2, 8)), dma((2, 8)),
            dma((RING,)), dma((RING,)),
        ],
        compiler_params=pltpu.CompilerParams(
            collective_id=0, has_side_effects=True, vmem_limit_bytes=48 * 1024 * 1024
        ),
    )(
        lengths, adapter_ids, hidden_input, norm_gain[None, :], table,
        adapter_up.reshape(ADAPTERS * RANK, B), routes.T, expert_in, jnp.transpose(expert_out, (0, 2, 1)),
    )


def solution(mesh):
    placed = (
        P("row", "col"),
        P("col"),
        P("col", None),
        P(None, None, "row", "col"),
        P(None, "col", "row"),
        P(None, "col", None),
        P(None, None, "col"),
        P("row", None),
        P(),
        P(),
    )
    return jax.shard_map(
        on_device, mesh=mesh, in_specs=placed, out_specs=P("row", "col"), check_vma=False
    )
```

```python
import jax
import jax.numpy as jnp
from jax import lax
from jax.experimental import pallas as pl
from jax.experimental.pallas import tpu as pltpu
from jax.sharding import PartitionSpec as P

NX, NZ, NC = 4, 4, 16
RING = 8
B = 128
D = 2048
F = 256
SLAB = 64
RANK, ADAPTERS, REQUESTS = 16, 16, 16
A_TWO = (5, 6, 7)
O_TWO = ()
FAR = (2,)
A_READY = (0.0, 4.0, 4.1, 5.0, 5.1, 6.5, 6.6, 8.0)
W_READY = (0.0, 8.5, 14.0, 9.0)
O_RING_AT = ((11.1, 7.4, 3.7, -2.0), (7.4, 3.7, -2.0))
O_TWO_AT = ((5.0, 6.0, 0.7, 0.5), (5.0, 6.0, 0.6))
O_LAST_AT = (15.0, 12.6)
O_SPREAD = 0.1
epsilon = 1e-05
adapter_scaling_factor = 2.0

MESH = pl.DeviceIdType.MESH
F32, BF16 = jnp.float32, jnp.bfloat16
HIGH = lax.Precision.HIGHEST
NT = (((1,), (1,)), ((), ()))
TN = (((0,), (0,)), ((), ()))


def kernel(
    lengths_hbm, ids_hbm, h_hbm, gain_hbm, router_hbm, down_hbm, up_hbm, routes_hbm, win_ref, wout_ref, out_ref,
    lengths, adapter_ids, h_ref, gain_ref, router_ref, down_ref, up_ref, routes_ref,
    xb, nb, wb, ob, hid, pr, pz, tr, inv_b, gate_b, pstage,
    rs_send, rs_recv, sm_send, sm_recv,
    acc, local_sem, sent, az_r, ab_r, wz_r, wx_r, wp_r, p_r, pz_r, t_r, rs_r, sm_r,
):
    row, col = lax.axis_index("row"), lax.axis_index("col")
    k = lax.rem(row, 2)
    chip_row = lax.div(row, 2)
    x, zh = lax.div(chip_row, NZ), lax.rem(chip_row, NZ)
    y, zl = lax.div(col, 2), lax.rem(col, 2)
    z = zh * 2 + zl
    big, small = y * (1 - k) + z * k, z * (1 - k) + y * k
    sy, sz = RING * (1 - k) + k, RING * k + (1 - k)

    def at_plane(b, s):
        yy, zz = b * (1 - k) + s * k, s * (1 - k) + b * k
        return ((x * NZ + lax.div(zz, 2)) * 2 + k, yy * 2 + lax.rem(zz, 2))

    def at_x(xx):
        return ((lax.rem(xx + NX, NX) * NZ + zh) * 2 + k, col)

    def ring(v):
        return lax.rem(v + RING, RING)

    partner = (chip_row * 2 + 1 - k, col)

    def send(src, dst, group, r_sem, device):
        pltpu.make_async_remote_copy(
            src_ref=src, dst_ref=dst, send_sem=sent.at[group], recv_sem=r_sem, device_id=device, device_id_type=MESH
        ).start()

    def waiter(ref, group, r_sem):
        return pltpu.make_async_remote_copy(
            src_ref=ref, dst_ref=ref, send_sem=sent.at[group], recv_sem=r_sem, device_id=partner, device_id_type=MESH
        )

    def arrived(dst, r_sem):
        waiter(dst, 0, r_sem).wait_recv()

    def rows_of(xx, jj):
        zz = lax.rem(zh - jj + NZ, NZ)
        r = (lax.rem(xx + NX, NX) * NZ + zz) * 2 + k
        return pl.ds(pl.multiple_of(r * SLAB, SLAB), SLAB)

    my_rows = rows_of(x, 0)
    mine = xb.at[big * RING + small]
    own_w = [
        pltpu.make_async_copy(win_ref.at[zh], wb.at[pl.ds(0, 2), my_rows], local_sem.at[1]),
        pltpu.make_async_copy(wout_ref.at[zh], wb.at[2, my_rows], local_sem.at[2]),
    ]
    blocks = [
        pltpu.make_async_copy(src, dst, local_sem.at[3 + i])
        for i, (src, dst) in enumerate((
            (h_hbm, h_ref), (gain_hbm, gain_ref), (router_hbm, router_ref), (down_hbm, down_ref),
            (lengths_hbm, lengths), (ids_hbm, adapter_ids), (routes_hbm, routes_ref), (up_hbm, up_ref),
        ))
    ]
    own_x = pltpu.make_async_copy(h_hbm, mine, local_sem.at[0])
    for copy in own_w + blocks + [own_x]:
        copy.start()

    peers = [at_plane(ring(big + d), small) for d in range(1, RING)]
    peers += [at_plane(big, ring(small + d)) for d in range(1, RING)]
    peers += [at_x(x + d) for d in range(1, NX)] + [partner]
    barrier = pltpu.get_barrier_semaphore()
    for peer in peers:
        pl.semaphore_signal(barrier, inc=1, device_id=peer, device_id_type=MESH)
    pl.semaphore_wait(barrier, len(peers))

    offsets = (0, 1, -1, 2, -2, 3, -3, 4)

    def a_block(b, offset):
        return xb.at[ring(b) * RING + ring(small - offset)]

    def a_long_send(i, start, way, to_distance):
        b = big - start if way == 0 else big + start
        ahead = to_distance - start
        to = at_plane(ring(big + ahead), small) if way == 0 else at_plane(ring(big - ahead), small)
        dst = a_block(b, offsets[i])
        src = h_hbm if i == 0 and start == 0 else dst
        send(src, dst, 1, ab_r.at[way, i, to_distance - 1], to)

    def onward(two, i, way, d):
        last = 4 if i % 2 == way else 3
        if two:
            served = {0: (1, 2), 2: (3, 4)}.get(d, ())
        else:
            served = (d + 1,)
        return [v for v in served if v <= last]

    def a_long(i, d, way):
        b = big - d if way == 0 else big + d
        if d:
            arrived(a_block(b, offsets[i]), ab_r.at[way, i, d - 1])
        for v in onward(i in A_TWO, i, way, d):
            a_long_send(i, d, way, v)

    def a_short(i):
        arrived(a_block(big, offsets[i]), az_r.at[i])
        for w in range(2):
            a_long(i, 0, w)

    for i in range(1, RING):
        send(h_hbm, mine, 0, az_r.at[i], at_plane(big, ring(small + offsets[i])))
    for w in range(2):
        a_long(0, 0, w)

    for j in (1, 3, 2):
        e = lax.rem(zh + j, NZ)
        to = ((x * NZ + e) * 2 + k, col)
        send(win_ref.at[e], wb.at[pl.ds(0, 2), my_rows], 2, wz_r.at[j], to)
        send(wout_ref.at[e], wb.at[2, my_rows], 2, wz_r.at[j], to)

    def w_piece(xx, j):
        return wb.at[:, rows_of(xx, j)]

    def w_out(xx, j, slot, right=False, left=False, far=False):
        piece = w_piece(xx, j)
        if right:
            m = j if slot == 0 else 4 + j
            send(piece, piece, 3, wx_r.at[0, m], at_x(x + 1))
        if left:
            m = j if slot == 0 else 4 + j
            send(piece, piece, 3, wx_r.at[1, m], at_x(x - 1))
        if far:
            side = 0 if j < 2 else 1
            send(piece, piece, 3, wx_r.at[side, 4 + j], at_x(x + 2))
        send(piece, piece, 4, wp_r.at[slot // 3], partner)

    def w_own(j):
        if j == 0:
            for copy in own_w:
                copy.wait()
        else:
            arrived(w_piece(x, j), wz_r.at[j])
        w_out(x, j, 0, right=True, left=True, far=j in FAR)

    def w_near(j, way):
        if way == 0:
            arrived(w_piece(x - 1, j), wx_r.at[0, j])
            w_out(x - 1, j, 1, right=j < 2 and j not in FAR)
        else:
            arrived(w_piece(x + 1, j), wx_r.at[1, j])
            w_out(x + 1, j, 2, left=j >= 2 and j not in FAR)

    def w_far(j):
        side = 0 if j < 2 else 1
        arrived(w_piece(x + 2, j), wx_r.at[side, 4 + j])
        w_out(x + 2, j, 3)

    w_own(0)

    for copy in blocks:
        copy.wait()
    hx = h_ref[...].astype(F32)
    ones = jnp.ones((8, B), F32)
    squares = lax.dot_general(ones, hx * hx, NT, precision=HIGH, preferred_element_type=F32)
    scaled = hx * gain_ref[...]
    projected = lax.dot_general(down_ref[...].astype(F32), scaled, NT, precision=HIGH, preferred_element_type=F32)
    routed = lax.dot_general(router_ref[...].astype(F32), scaled, NT, precision=HIGH, preferred_element_type=F32)
    line = lax.broadcasted_iota(jnp.int32, (8, B), 0)
    tile = squares
    for e in range(NZ):
        tile = jnp.where(line == 1 + e, jnp.broadcast_to(routed[e : e + 1], (8, B)), tile)
    tile = jnp.where(line >= 5, 0.0, tile)
    tile = jnp.where(line == 5 + zl, jnp.broadcast_to(gain_ref[...], (8, B)), tile)
    position = row * B + lax.broadcasted_iota(jnp.int32, (1, B), 1)
    bound = lengths[0]
    request = (position >= bound).astype(jnp.int32)
    for i in range(1, REQUESTS):
        bound = bound + lengths[i]
        request = request + (position >= bound).astype(jnp.int32)
    adapter = jnp.zeros((1, B), jnp.int32)
    for i in range(REQUESTS):
        adapter = jnp.where(request == i, adapter_ids[i], adapter)
    adapter = jnp.broadcast_to(adapter, (RANK, B))
    part = jnp.zeros((RANK, B), F32)
    for a in range(ADAPTERS):
        part = part + jnp.where(adapter == a, projected[a * RANK : (a + 1) * RANK], 0.0)
    pstage[0, 0:8] = tile
    pstage[0, 8:24] = part
    other = (row, y * 2 + 1 - zl)
    send(pstage.at[0], pz, 6, pz_r.at[0], other)

    def pair_event():
        arrived(pz, pz_r.at[0])
        both = pz[...] + jnp.concatenate([tile, part], axis=0)
        pstage[1] = both
        pr[y] = both
        for d in range(1, RING):
            send(pstage.at[1], pr.at[y], 5, p_r.at[0], (row, ring(y + d) * 2 + zl))

    def gates_event():
        arrived(pr.at[pl.ds(0, RING - 1)], p_r.at[0])
        total = pr[0]
        for i in range(1, RING):
            total = total + pr[i]
        inverse = lax.rsqrt(total[0:1] / D + epsilon)
        logits = [total[1 + e : 2 + e] * inverse for e in range(NZ)]
        route = [routes_ref[0:1, :], routes_ref[1:2, :]]
        chosen = []
        for i in range(2):
            value = jnp.zeros((1, B), F32)
            for e in range(NZ):
                value = jnp.where(route[i] == e, logits[e], value)
            chosen.append(value)
        gates = [jax.nn.sigmoid(chosen[0] - chosen[1]), jax.nn.sigmoid(chosen[1] - chosen[0])]
        share = jnp.where(line == 0, jnp.broadcast_to(inverse, (8, B)), 0.0)
        for e in range(NZ):
            weight = jnp.where(route[0] == e, gates[0], 0.0) + jnp.where(route[1] == e, gates[1], 0.0)
            share = jnp.where(line == 1 + e, jnp.broadcast_to(weight, (8, B)), share)
        tr[zh] = share
        for d in range(1, NZ):
            to = ((x * NZ + lax.rem(zh + d, NZ)) * 2 + k, col)
            send(tr.at[zh], tr.at[zh], 7, t_r.at[0], to)
        return inverse, total[8:24] * jnp.broadcast_to(inverse, (RANK, B))

    def columns_event():
        arrived(tr.at[pl.ds(0, NZ - 1)], t_r.at[0])
        for i in range(NZ):
            rows = tr[i]
            gate_row = tr[i, pl.ds(1 + zh, 1), :]
            both = jnp.where(line == 0, rows, jnp.broadcast_to(gate_row, (8, B)))
            turned = jnp.transpose(both)
            inv_b[i] = jnp.broadcast_to(turned[:, 0:1], (B, B))
            gate_b[i] = jnp.broadcast_to(turned[:, 1:2], (B, B))

    events = [(5.0, pair_event, ()), (11.0, gates_event, ()), (16.0, columns_event, ())]
    for i in range(RING):
        ready = A_READY[i]
        if i:
            events.append((ready, a_short, (i,)))
        for way in range(2):
            for d in range(1, 5 if i % 2 == way else 4):
                hops = ((d + 1) // 2 if i in A_TWO else d)
                events.append((ready + 3.5 * hops, a_long, (i, d, way)))
    for j, ready in enumerate(W_READY):
        for way in range(2):
            events.append((ready + 4.0, w_near, (j, way)))
        if j:
            events.append((ready, w_own, (j,)))
        events.append((ready + (5.0 if j in FAR else 8.0), w_far, (j,)))
    kept = {}
    for _, action, given in sorted(events, key=lambda event: event[0]):
        kept[action] = action(*given)
    latent = kept[gates_event][1]
    own_x.wait()

    @pl.loop(0, RING * RING)
    def _(i):
        yy, zz = lax.div(i, RING), lax.rem(i, RING)
        c, t = yy * 2 + lax.rem(zz, 2), lax.div(zz, 2)
        value = xb[yy * sy + zz * sz].astype(F32) * inv_b[t] * pr[yy, pl.ds(5 + lax.rem(zz, 2), 1), :]
        nb[pl.ds(pl.multiple_of(t * B, B), B), pl.ds(pl.multiple_of(c * B, B), B)] = value.astype(BF16)

    def contract(step, xx):
        part = pl.ds(pl.multiple_of(lax.rem(xx + NX, NX) * 512, 512), 512)

        @pl.loop(0, 2)
        def _(i):
            rows = pl.ds(pl.multiple_of(i * 256, 256), 256)
            tokens = nb[rows, part]
            sums = [jnp.dot(tokens, wb[n, part, :], preferred_element_type=F32) for n in range(2)]
            if step:
                sums = [acc[n, rows, :] + sums[n] for n in range(2)]
            if step < 3:
                for n in range(2):
                    acc[n, rows, :] = sums[n]
            else:
                hid[rows, :] = (jax.nn.silu(sums[0]) * sums[1]).astype(BF16)

    arrived(wb.at[:, pl.ds(0, 12 * SLAB)], wp_r.at[0])
    for step in range(3):
        contract(step, (x, x - 1, x + 1)[step])
    arrived(wb.at[:, pl.ds(0, 4 * SLAB)], wp_r.at[1])
    contract(3, x + 2)

    @pl.loop(0, RING)
    def _(yy):
        weights = wb[2, pl.ds(pl.multiple_of(yy * 256, 256), 256), :]
        result = lax.dot_general(hid[...], weights, NT, preferred_element_type=F32)
        for t in range(NZ):
            for half in range(2):
                block = result[t * B : (t + 1) * B, half * B : (half + 1) * B]
                ob[yy * sy + (t * 2 + half) * sz] = block * gate_b[t]

    targets = (4, 3, -3, 2, -2, 1, -1, 0)

    def r_sum(i, j, way, value):
        arrived(rs_recv.at[(way * RING + i) * 4 + j - 1], rs_r.at[way, i, j - 1])
        return value + rs_recv[(way * RING + i) * 4 + j - 1].astype(F32)

    def r_send(i, j, way):
        b = ring(big + j) if way == 0 else ring(big - j)
        value = ob[b * RING + ring(small + targets[i])]
        last = 4 if i % 2 == way else 3
        if i in O_TWO:
            sources = [v for v in (3, 4) if v <= last] if j == 2 else []
            ahead = {1: 1, 2: 2, 3: 1, 4: 2}[j]
        else:
            sources = [j + 1] if j < last else []
            ahead = 1
        for v in sources:
            value = r_sum(i, v, way, value)
        rs_send[(way * RING + i) * 4 + j - 1] = value.astype(BF16)
        to = at_plane(ring(big + ahead), small) if way == 0 else at_plane(ring(big - ahead), small)
        send(rs_send.at[(way * RING + i) * 4 + j - 1], rs_recv.at[(way * RING + i) * 4 + j - 1], 8, rs_r.at[way, i, j - 1], to)

    def r_last(i):
        s = ring(small + targets[i])
        value = ob[big * RING + s]
        for way in range(2):
            for v in (1, 2) if i in O_TWO else (1,):
                value = r_sum(i, v, way, value)
        if targets[i]:
            sm_send[i] = value.astype(BF16)
            send(sm_send.at[i], sm_recv.at[i], 9, sm_r.at[0], at_plane(big, s))
        return value

    def delta_event():
        spread = jnp.concatenate([jnp.where(adapter == a, latent, 0.0) for a in range(ADAPTERS)], axis=0)
        delta = lax.dot_general(spread, up_ref[...].astype(F32), TN, precision=HIGH, preferred_element_type=F32)
        return delta

    events = [(7.0, delta_event, ())]
    for i in range(RING):
        for way in range(2):
            first = 4 if i % 2 == way else 3
            for j in range(1, first + 1):
                when = (O_TWO_AT if i in O_TWO else O_RING_AT)[first == 3][j - 1] + O_SPREAD * i
                events.append((when, r_send, (i, j, way)))
        events.append((O_LAST_AT[i in O_TWO] + O_SPREAD * i, r_last, (i,)))
    for _, action, given in sorted(events, key=lambda event: event[0]):
        kept[action] = action(*given)
    result = kept[r_last] + adapter_scaling_factor * kept[delta_event]
    arrived(sm_recv.at[pl.ds(0, RING - 1)], sm_r.at[0])
    for i in range(RING - 1):
        result = result + sm_recv[i].astype(F32)
    out_ref[...] = result.astype(BF16)
    for group, ref in enumerate((
        xb.at[pl.ds(0, 7)], xb.at[pl.ds(0, 56)], wb.at[:, pl.ds(0, 3 * SLAB)], wb.at[:, pl.ds(0, 12 * SLAB)],
        wb.at[:, pl.ds(0, 16 * SLAB)], pr.at[pl.ds(0, 7)], pz, tr.at[pl.ds(0, 3)],
        rs_send.at[pl.ds(0, 56)], sm_send.at[pl.ds(0, 7)],
    )):
        waiter(ref, group, pz_r.at[0]).wait_send()


def on_device(
    hidden_input, norm_gain, router_weight, expert_in, expert_out, adapter_down, adapter_up, routes, lengths, adapter_ids
):
    down = jnp.transpose(adapter_down, (0, 2, 1)).reshape(ADAPTERS * RANK, B)
    vmem = pl.BlockSpec(memory_space=pltpu.VMEM)
    hbm = pl.BlockSpec(memory_space=pltpu.HBM)
    dma = pltpu.SemaphoreType.DMA
    return pl.pallas_call(
        kernel,
        out_shape=jax.ShapeDtypeStruct((B, B), BF16),
        in_specs=[hbm] * 10,
        out_specs=vmem,
        scratch_shapes=[
            pltpu.SMEM((REQUESTS,), jnp.int32),
            pltpu.SMEM((REQUESTS,), jnp.int32),
            pltpu.VMEM((B, B), BF16),
            pltpu.VMEM((1, B), F32),
            pltpu.VMEM((NZ, B), BF16),
            pltpu.VMEM((ADAPTERS * RANK, B), BF16),
            pltpu.VMEM((ADAPTERS * RANK, B), BF16),
            pltpu.VMEM((2, B), jnp.int32),
            pltpu.VMEM((RING * RING, B, B), BF16),
            pltpu.VMEM((NZ * B, D), BF16),
            pltpu.VMEM((3, D, F), BF16),
            pltpu.VMEM((RING * RING, B, B), F32),
            pltpu.VMEM((NZ * B, F), BF16),
            pltpu.VMEM((RING, 24, B), F32),
            pltpu.VMEM((24, B), F32),
            pltpu.VMEM((NZ, 8, B), F32),
            pltpu.VMEM((NZ, B, B), F32),
            pltpu.VMEM((NZ, B, B), F32),
            pltpu.VMEM((2, 24, B), F32),
            pltpu.VMEM((8 * RING, B, B), BF16),
            pltpu.VMEM((8 * RING, B, B), BF16),
            pltpu.VMEM((RING, B, B), BF16),
            pltpu.VMEM((RING, B, B), BF16),
            pltpu.VMEM((2, NZ * B, F), F32),
            dma((11,)),
            dma((10,)),
            dma((RING,)),
            dma((2, RING, 4)),
            dma((NZ,)),
            dma((2, 8)),
            dma((2,)),
            dma((1,)), dma((1,)), dma((1,)),
            dma((2, RING, 4)),
            dma((1,)),
        ],
        compiler_params=pltpu.CompilerParams(
            collective_id=0, has_side_effects=True
        ),
    )(
        lengths, adapter_ids, hidden_input, norm_gain[None, :], router_weight.T, down,
        adapter_up.reshape(ADAPTERS * RANK, B), routes.T, expert_in, jnp.transpose(expert_out, (0, 2, 1)),
    )


def solution(mesh):
    placed = (
        P("row", "col"),
        P("col"),
        P("col", None),
        P(None, None, "row", "col"),
        P(None, "col", "row"),
        P(None, "col", None),
        P(None, None, "col"),
        P("row", None),
        P(),
        P(),
    )
    return jax.shard_map(
        on_device, mesh=mesh, in_specs=placed, out_specs=P("row", "col"), check_vma=False
    )
```

```python
import jax
import jax.numpy as jnp
from jax import lax
from jax.experimental import pallas as pl
from jax.experimental.pallas import tpu as pltpu
from jax.sharding import PartitionSpec as P

NX, NZ, NC = 4, 4, 16
RING = 8
B = 128
D = 2048
F = 256
SLAB = 64
RANK, ADAPTERS, REQUESTS = 16, 16, 16
A_TWO = (5, 6, 7)
O_TWO = ()
FAR = (2,)
A_READY = (0.0, 5.0, 5.1, 6.0, 6.1, 7.0, 7.1, 8.5)
W_READY = (0.0, 8.5, 14.0, 9.0)
O_RING_AT = ((11.1, 7.4, 3.7, -2.0), (7.4, 3.7, -2.0))
O_TWO_AT = ((5.0, 6.0, 0.7, 0.5), (5.0, 6.0, 0.6))
O_LAST_AT = (15.0, 12.6)
O_SPREAD = 0.1
P_AT = (9.0, 17.0, 26.0)
A_HOP = 3.9
W_AFTER = (4.0, 5.0, 8.0)
epsilon = 1e-05
adapter_scaling_factor = 2.0

MESH = pl.DeviceIdType.MESH
F32, BF16 = jnp.float32, jnp.bfloat16
HIGH = lax.Precision.HIGHEST
NT = (((1,), (1,)), ((), ()))
TN = (((0,), (0,)), ((), ()))


def kernel(
    lengths_hbm, ids_hbm, h_hbm, gain_hbm, router_hbm, down_hbm, up_hbm, routes_hbm, win_ref, wout_ref, out_ref,
    lengths, adapter_ids, h_ref, gain_ref, router_ref, down_ref, up_ref, routes_ref,
    xb, nb, wb, ob, hid, pr, pz, tr, inv_b, gate_b, pstage,
    rs_send, rs_recv, sm_send, sm_recv,
    acc, local_sem, sent, az_r, ab_r, wz_r, wx_r, wp_r, p_r, pz_r, t_r, rs_r, sm_r,
):
    row, col = lax.axis_index("row"), lax.axis_index("col")
    k = lax.rem(row, 2)
    chip_row = lax.div(row, 2)
    x, zh = lax.div(chip_row, NZ), lax.rem(chip_row, NZ)
    y, zl = lax.div(col, 2), lax.rem(col, 2)
    z = zh * 2 + zl
    big, small = y * (1 - k) + z * k, z * (1 - k) + y * k
    sy, sz = RING * (1 - k) + k, RING * k + (1 - k)

    def at_plane(b, s):
        yy, zz = b * (1 - k) + s * k, s * (1 - k) + b * k
        return ((x * NZ + lax.div(zz, 2)) * 2 + k, yy * 2 + lax.rem(zz, 2))

    def at_x(xx):
        return ((lax.rem(xx + NX, NX) * NZ + zh) * 2 + k, col)

    def ring(v):
        return lax.rem(v + RING, RING)

    partner = (chip_row * 2 + 1 - k, col)

    def send(src, dst, group, r_sem, device):
        pltpu.make_async_remote_copy(
            src_ref=src, dst_ref=dst, send_sem=sent.at[group], recv_sem=r_sem, device_id=device, device_id_type=MESH
        ).start()

    def waiter(ref, group, r_sem):
        return pltpu.make_async_remote_copy(
            src_ref=ref, dst_ref=ref, send_sem=sent.at[group], recv_sem=r_sem, device_id=partner, device_id_type=MESH
        )

    def arrived(dst, r_sem):
        waiter(dst, 0, r_sem).wait_recv()

    def rows_of(xx, jj):
        zz = lax.rem(zh - jj + NZ, NZ)
        r = (lax.rem(xx + NX, NX) * NZ + zz) * 2 + k
        return pl.ds(pl.multiple_of(r * SLAB, SLAB), SLAB)

    my_rows = rows_of(x, 0)
    mine = xb.at[big * RING + small]
    own_w = [
        pltpu.make_async_copy(win_ref.at[zh], wb.at[pl.ds(0, 2), my_rows], local_sem.at[1]),
        pltpu.make_async_copy(wout_ref.at[zh], wb.at[2, my_rows], local_sem.at[2]),
    ]
    blocks = [
        pltpu.make_async_copy(src, dst, local_sem.at[3 + i])
        for i, (src, dst) in enumerate((
            (h_hbm, h_ref), (gain_hbm, gain_ref), (router_hbm, router_ref), (down_hbm, down_ref),
            (lengths_hbm, lengths), (ids_hbm, adapter_ids), (routes_hbm, routes_ref), (up_hbm, up_ref),
        ))
    ]
    own_x = pltpu.make_async_copy(h_hbm, mine, local_sem.at[0])
    for copy in own_w + blocks + [own_x]:
        copy.start()

    peers = [at_plane(ring(big + d), small) for d in range(1, RING)]
    peers += [at_plane(big, ring(small + d)) for d in range(1, RING)]
    peers += [at_x(x + d) for d in range(1, NX)] + [partner]
    barrier = pltpu.get_barrier_semaphore()
    for peer in peers:
        pl.semaphore_signal(barrier, inc=1, device_id=peer, device_id_type=MESH)
    pl.semaphore_wait(barrier, len(peers))

    offsets = (0, 1, -1, 2, -2, 3, -3, 4)

    def a_block(b, offset):
        return xb.at[ring(b) * RING + ring(small - offset)]

    def a_long_send(i, start, way, to_distance):
        b = big - start if way == 0 else big + start
        ahead = to_distance - start
        to = at_plane(ring(big + ahead), small) if way == 0 else at_plane(ring(big - ahead), small)
        dst = a_block(b, offsets[i])
        src = h_hbm if i == 0 and start == 0 else dst
        send(src, dst, 1, ab_r.at[way, i, to_distance - 1], to)

    def onward(two, i, way, d):
        last = 4 if i % 2 == way else 3
        if two:
            served = {0: (1, 2), 2: (3, 4)}.get(d, ())
        else:
            served = (d + 1,)
        return [v for v in served if v <= last]

    def a_long(i, d, way):
        b = big - d if way == 0 else big + d
        if d:
            arrived(a_block(b, offsets[i]), ab_r.at[way, i, d - 1])
        for v in onward(i in A_TWO, i, way, d):
            a_long_send(i, d, way, v)

    def a_short(i):
        arrived(a_block(big, offsets[i]), az_r.at[i])
        for w in range(2):
            a_long(i, 0, w)

    for i in range(1, RING):
        send(h_hbm, mine, 0, az_r.at[i], at_plane(big, ring(small + offsets[i])))
    for w in range(2):
        a_long(0, 0, w)

    for j in (1, 3, 2):
        e = lax.rem(zh + j, NZ)
        to = ((x * NZ + e) * 2 + k, col)
        send(win_ref.at[e], wb.at[pl.ds(0, 2), my_rows], 2, wz_r.at[j], to)
        send(wout_ref.at[e], wb.at[2, my_rows], 2, wz_r.at[j], to)

    def w_piece(xx, j):
        return wb.at[:, rows_of(xx, j)]

    def w_out(xx, j, slot, right=False, left=False, far=False):
        piece = w_piece(xx, j)
        if right:
            m = j if slot == 0 else 4 + j
            send(piece, piece, 3, wx_r.at[0, m], at_x(x + 1))
        if left:
            m = j if slot == 0 else 4 + j
            send(piece, piece, 3, wx_r.at[1, m], at_x(x - 1))
        if far:
            side = 0 if j < 2 else 1
            send(piece, piece, 3, wx_r.at[side, 4 + j], at_x(x + 2))
        send(piece, piece, 4, wp_r.at[slot // 3], partner)

    def w_own(j):
        if j == 0:
            for copy in own_w:
                copy.wait()
        else:
            arrived(w_piece(x, j), wz_r.at[j])
        w_out(x, j, 0, right=True, left=True, far=j in FAR)

    def w_near(j, way):
        if way == 0:
            arrived(w_piece(x - 1, j), wx_r.at[0, j])
            w_out(x - 1, j, 1, right=j < 2 and j not in FAR)
        else:
            arrived(w_piece(x + 1, j), wx_r.at[1, j])
            w_out(x + 1, j, 2, left=j >= 2 and j not in FAR)

    def w_far(j):
        side = 0 if j < 2 else 1
        arrived(w_piece(x + 2, j), wx_r.at[side, 4 + j])
        w_out(x + 2, j, 3)

    w_own(0)

    for copy in blocks:
        copy.wait()
    hx = h_ref[...].astype(F32)
    ones = jnp.ones((8, B), F32)
    squares = lax.dot_general(ones, hx * hx, NT, precision=HIGH, preferred_element_type=F32)
    scaled = hx * gain_ref[...]
    projected = lax.dot_general(down_ref[...].astype(F32), scaled, NT, precision=HIGH, preferred_element_type=F32)
    routed = lax.dot_general(router_ref[...].astype(F32), scaled, NT, precision=HIGH, preferred_element_type=F32)
    line = lax.broadcasted_iota(jnp.int32, (8, B), 0)
    tile = squares
    for e in range(NZ):
        tile = jnp.where(line == 1 + e, jnp.broadcast_to(routed[e : e + 1], (8, B)), tile)
    tile = jnp.where(line >= 5, 0.0, tile)
    tile = jnp.where(line == 5 + zl, jnp.broadcast_to(gain_ref[...], (8, B)), tile)
    position = row * B + lax.broadcasted_iota(jnp.int32, (1, B), 1)
    bound = lengths[0]
    request = (position >= bound).astype(jnp.int32)
    for i in range(1, REQUESTS):
        bound = bound + lengths[i]
        request = request + (position >= bound).astype(jnp.int32)
    adapter = jnp.zeros((1, B), jnp.int32)
    for i in range(REQUESTS):
        adapter = jnp.where(request == i, adapter_ids[i], adapter)
    adapter = jnp.broadcast_to(adapter, (RANK, B))
    part = jnp.zeros((RANK, B), F32)
    for a in range(ADAPTERS):
        part = part + jnp.where(adapter == a, projected[a * RANK : (a + 1) * RANK], 0.0)
    pstage[0, 0:8] = tile
    pstage[0, 8:24] = part
    other = (row, y * 2 + 1 - zl)
    send(pstage.at[0], pz, 6, pz_r.at[0], other)

    def pair_event():
        arrived(pz, pz_r.at[0])
        both = pz[...] + jnp.concatenate([tile, part], axis=0)
        pstage[1] = both
        pr[y] = both
        for d in range(1, RING):
            send(pstage.at[1], pr.at[y], 5, p_r.at[0], (row, ring(y + d) * 2 + zl))

    def gates_event():
        arrived(pr.at[pl.ds(0, RING - 1)], p_r.at[0])
        total = pr[0]
        for i in range(1, RING):
            total = total + pr[i]
        inverse = lax.rsqrt(total[0:1] / D + epsilon)
        logits = [total[1 + e : 2 + e] * inverse for e in range(NZ)]
        route = [routes_ref[0:1, :], routes_ref[1:2, :]]
        chosen = []
        for i in range(2):
            value = jnp.zeros((1, B), F32)
            for e in range(NZ):
                value = jnp.where(route[i] == e, logits[e], value)
            chosen.append(value)
        gates = [jax.nn.sigmoid(chosen[0] - chosen[1]), jax.nn.sigmoid(chosen[1] - chosen[0])]
        share = jnp.where(line == 0, jnp.broadcast_to(inverse, (8, B)), 0.0)
        for e in range(NZ):
            weight = jnp.where(route[0] == e, gates[0], 0.0) + jnp.where(route[1] == e, gates[1], 0.0)
            share = jnp.where(line == 1 + e, jnp.broadcast_to(weight, (8, B)), share)
        tr[zh] = share
        for d in range(1, NZ):
            to = ((x * NZ + lax.rem(zh + d, NZ)) * 2 + k, col)
            send(tr.at[zh], tr.at[zh], 7, t_r.at[0], to)
        return inverse, total[8:24] * jnp.broadcast_to(inverse, (RANK, B))

    def columns_event():
        arrived(tr.at[pl.ds(0, NZ - 1)], t_r.at[0])
        for i in range(NZ):
            rows = tr[i]
            gate_row = tr[i, pl.ds(1 + zh, 1), :]
            both = jnp.where(line == 0, rows, jnp.broadcast_to(gate_row, (8, B)))
            turned = jnp.transpose(both)
            inv_b[i] = jnp.broadcast_to(turned[:, 0:1], (B, B))
            gate_b[i] = jnp.broadcast_to(turned[:, 1:2], (B, B))

    events = [(P_AT[0], pair_event, ()), (P_AT[1], gates_event, ()), (P_AT[2], columns_event, ())]
    for i in range(RING):
        ready = A_READY[i]
        if i:
            events.append((ready, a_short, (i,)))
        for way in range(2):
            for d in range(1, 5 if i % 2 == way else 4):
                hops = ((d + 1) // 2 if i in A_TWO else d)
                events.append((ready + A_HOP * hops, a_long, (i, d, way)))
    for j, ready in enumerate(W_READY):
        for way in range(2):
            events.append((ready + W_AFTER[0], w_near, (j, way)))
        if j:
            events.append((ready, w_own, (j,)))
        events.append((ready + (W_AFTER[1] if j in FAR else W_AFTER[2]), w_far, (j,)))
    kept = {}
    for _, action, given in sorted(events, key=lambda event: event[0]):
        kept[action] = action(*given)
    latent = kept[gates_event][1]
    own_x.wait()

    @pl.loop(0, RING * RING)
    def _(i):
        yy, zz = lax.div(i, RING), lax.rem(i, RING)
        c, t = yy * 2 + lax.rem(zz, 2), lax.div(zz, 2)
        value = xb[yy * sy + zz * sz].astype(F32) * inv_b[t] * pr[yy, pl.ds(5 + lax.rem(zz, 2), 1), :]
        nb[pl.ds(pl.multiple_of(t * B, B), B), pl.ds(pl.multiple_of(c * B, B), B)] = value.astype(BF16)

    def contract(step, xx):
        part = pl.ds(pl.multiple_of(lax.rem(xx + NX, NX) * 512, 512), 512)

        @pl.loop(0, 2)
        def _(i):
            rows = pl.ds(pl.multiple_of(i * 256, 256), 256)
            tokens = nb[rows, part]
            sums = [jnp.dot(tokens, wb[n, part, :], preferred_element_type=F32) for n in range(2)]
            if step:
                sums = [acc[n, rows, :] + sums[n] for n in range(2)]
            if step < 3:
                for n in range(2):
                    acc[n, rows, :] = sums[n]
            else:
                hid[rows, :] = (jax.nn.silu(sums[0]) * sums[1]).astype(BF16)

    arrived(wb.at[:, pl.ds(0, 12 * SLAB)], wp_r.at[0])
    for step in range(3):
        contract(step, (x, x - 1, x + 1)[step])
    arrived(wb.at[:, pl.ds(0, 4 * SLAB)], wp_r.at[1])
    contract(3, x + 2)

    @pl.loop(0, RING)
    def _(yy):
        weights = wb[2, pl.ds(pl.multiple_of(yy * 256, 256), 256), :]
        result = lax.dot_general(hid[...], weights, NT, preferred_element_type=F32)
        for t in range(NZ):
            for half in range(2):
                block = result[t * B : (t + 1) * B, half * B : (half + 1) * B]
                ob[yy * sy + (t * 2 + half) * sz] = block * gate_b[t]

    targets = (4, 3, -3, 2, -2, 1, -1, 0)

    def r_sum(i, j, way, value):
        arrived(rs_recv.at[(way * RING + i) * 4 + j - 1], rs_r.at[way, i, j - 1])
        return value + rs_recv[(way * RING + i) * 4 + j - 1].astype(F32)

    def r_send(i, j, way):
        b = ring(big + j) if way == 0 else ring(big - j)
        value = ob[b * RING + ring(small + targets[i])]
        last = 4 if i % 2 == way else 3
        if i in O_TWO:
            sources = [v for v in (3, 4) if v <= last] if j == 2 else []
            ahead = {1: 1, 2: 2, 3: 1, 4: 2}[j]
        else:
            sources = [j + 1] if j < last else []
            ahead = 1
        for v in sources:
            value = r_sum(i, v, way, value)
        rs_send[(way * RING + i) * 4 + j - 1] = value.astype(BF16)
        to = at_plane(ring(big + ahead), small) if way == 0 else at_plane(ring(big - ahead), small)
        send(rs_send.at[(way * RING + i) * 4 + j - 1], rs_recv.at[(way * RING + i) * 4 + j - 1], 8, rs_r.at[way, i, j - 1], to)

    def r_last(i):
        s = ring(small + targets[i])
        value = ob[big * RING + s]
        for way in range(2):
            for v in (1, 2) if i in O_TWO else (1,):
                value = r_sum(i, v, way, value)
        if targets[i]:
            sm_send[i] = value.astype(BF16)
            send(sm_send.at[i], sm_recv.at[i], 9, sm_r.at[0], at_plane(big, s))
        return value

    def delta_event():
        spread = jnp.concatenate([jnp.where(adapter == a, latent, 0.0) for a in range(ADAPTERS)], axis=0)
        delta = lax.dot_general(spread, up_ref[...].astype(F32), TN, precision=HIGH, preferred_element_type=F32)
        return delta

    events = [(7.0, delta_event, ())]
    for i in range(RING):
        for way in range(2):
            first = 4 if i % 2 == way else 3
            for j in range(1, first + 1):
                when = (O_TWO_AT if i in O_TWO else O_RING_AT)[first == 3][j - 1] + O_SPREAD * i
                events.append((when, r_send, (i, j, way)))
        events.append((O_LAST_AT[i in O_TWO] + O_SPREAD * i, r_last, (i,)))
    for _, action, given in sorted(events, key=lambda event: event[0]):
        kept[action] = action(*given)
    result = kept[r_last] + adapter_scaling_factor * kept[delta_event]
    arrived(sm_recv.at[pl.ds(0, RING - 1)], sm_r.at[0])
    for i in range(RING - 1):
        result = result + sm_recv[i].astype(F32)
    out_ref[...] = result.astype(BF16)
    for group, ref in enumerate((
        xb.at[pl.ds(0, 7)], xb.at[pl.ds(0, 56)], wb.at[:, pl.ds(0, 3 * SLAB)], wb.at[:, pl.ds(0, 12 * SLAB)],
        wb.at[:, pl.ds(0, 16 * SLAB)], pr.at[pl.ds(0, 7)], pz, tr.at[pl.ds(0, 3)],
        rs_send.at[pl.ds(0, 56)], sm_send.at[pl.ds(0, 7)],
    )):
        waiter(ref, group, pz_r.at[0]).wait_send()


def on_device(
    hidden_input, norm_gain, router_weight, expert_in, expert_out, adapter_down, adapter_up, routes, lengths, adapter_ids
):
    down = jnp.transpose(adapter_down, (0, 2, 1)).reshape(ADAPTERS * RANK, B)
    vmem = pl.BlockSpec(memory_space=pltpu.VMEM)
    hbm = pl.BlockSpec(memory_space=pltpu.HBM)
    dma = pltpu.SemaphoreType.DMA
    return pl.pallas_call(
        kernel,
        out_shape=jax.ShapeDtypeStruct((B, B), BF16),
        in_specs=[hbm] * 10,
        out_specs=vmem,
        scratch_shapes=[
            pltpu.SMEM((REQUESTS,), jnp.int32),
            pltpu.SMEM((REQUESTS,), jnp.int32),
            pltpu.VMEM((B, B), BF16),
            pltpu.VMEM((1, B), F32),
            pltpu.VMEM((NZ, B), BF16),
            pltpu.VMEM((ADAPTERS * RANK, B), BF16),
            pltpu.VMEM((ADAPTERS * RANK, B), BF16),
            pltpu.VMEM((2, B), jnp.int32),
            pltpu.VMEM((RING * RING, B, B), BF16),
            pltpu.VMEM((NZ * B, D), BF16),
            pltpu.VMEM((3, D, F), BF16),
            pltpu.VMEM((RING * RING, B, B), F32),
            pltpu.VMEM((NZ * B, F), BF16),
            pltpu.VMEM((RING, 24, B), F32),
            pltpu.VMEM((24, B), F32),
            pltpu.VMEM((NZ, 8, B), F32),
            pltpu.VMEM((NZ, B, B), F32),
            pltpu.VMEM((NZ, B, B), F32),
            pltpu.VMEM((2, 24, B), F32),
            pltpu.VMEM((8 * RING, B, B), BF16),
            pltpu.VMEM((8 * RING, B, B), BF16),
            pltpu.VMEM((RING, B, B), BF16),
            pltpu.VMEM((RING, B, B), BF16),
            pltpu.VMEM((2, NZ * B, F), F32),
            dma((11,)),
            dma((10,)),
            dma((RING,)),
            dma((2, RING, 4)),
            dma((NZ,)),
            dma((2, 8)),
            dma((2,)),
            dma((1,)), dma((1,)), dma((1,)),
            dma((2, RING, 4)),
            dma((1,)),
        ],
        compiler_params=pltpu.CompilerParams(
            collective_id=0, has_side_effects=True
        ),
    )(
        lengths, adapter_ids, hidden_input, norm_gain[None, :], router_weight.T, down,
        adapter_up.reshape(ADAPTERS * RANK, B), routes.T, expert_in, jnp.transpose(expert_out, (0, 2, 1)),
    )


def solution(mesh):
    placed = (
        P("row", "col"),
        P("col"),
        P("col", None),
        P(None, None, "row", "col"),
        P(None, "col", "row"),
        P(None, "col", None),
        P(None, None, "col"),
        P("row", None),
        P(),
        P(),
    )
    return jax.shard_map(
        on_device, mesh=mesh, in_specs=placed, out_specs=P("row", "col"), check_vma=False
    )
```

```python
import jax
import jax.numpy as jnp
from jax import lax
from jax.experimental import pallas as pl
from jax.experimental.pallas import tpu as pltpu
from jax.sharding import PartitionSpec as P

NX, NZ, NC = 4, 4, 16
RING = 8
B = 128
D = 2048
F = 256
SLAB = 64
RANK, ADAPTERS, REQUESTS = 16, 16, 16
A_TWO = (5, 6, 7)
O_TWO = (0, 1, 2)
FAR = (2,)
A_READY = (0.0, 5.0, 5.1, 6.0, 6.1, 7.0, 7.1, 8.5)
W_READY = (0.0, 8.5, 14.0, 9.0)
O_RING_AT = ((11.1, 7.4, 3.7, -2.0), (7.4, 3.7, -2.0))
O_TWO_AT = ((8.3, 5.8, 0.7, 0.5), (8.3, 5.8, 0.6))
O_LAST_AT = (15.0, 13.2)
O_SPREAD = 0.1
P_AT = (9.0, 17.0, 26.0)
A_HOP = 3.9
W_AFTER = (4.0, 5.0, 8.0)
epsilon = 1e-05
adapter_scaling_factor = 2.0

MESH = pl.DeviceIdType.MESH
F32, BF16 = jnp.float32, jnp.bfloat16
HIGH = lax.Precision.HIGHEST
NT = (((1,), (1,)), ((), ()))
TN = (((0,), (0,)), ((), ()))


def kernel(
    lengths_hbm, ids_hbm, h_hbm, gain_hbm, router_hbm, down_hbm, up_hbm, routes_hbm, win_ref, wout_ref, out_ref,
    lengths, adapter_ids, h_ref, gain_ref, router_ref, down_ref, up_ref, routes_ref,
    xb, nb, wb, ob, hid, pr, pz, tr, inv_b, gate_b, pstage,
    rs_send, rs_recv, sm_send, sm_recv,
    acc, local_sem, sent, az_r, ab_r, wz_r, wx_r, wp_r, p_r, pz_r, t_r, rs_r, sm_r,
):
    row, col = lax.axis_index("row"), lax.axis_index("col")
    k = lax.rem(row, 2)
    chip_row = lax.div(row, 2)
    x, zh = lax.div(chip_row, NZ), lax.rem(chip_row, NZ)
    y, zl = lax.div(col, 2), lax.rem(col, 2)
    z = zh * 2 + zl
    big, small = y * (1 - k) + z * k, z * (1 - k) + y * k
    sy, sz = RING * (1 - k) + k, RING * k + (1 - k)

    def at_plane(b, s):
        yy, zz = b * (1 - k) + s * k, s * (1 - k) + b * k
        return ((x * NZ + lax.div(zz, 2)) * 2 + k, yy * 2 + lax.rem(zz, 2))

    def at_x(xx):
        return ((lax.rem(xx + NX, NX) * NZ + zh) * 2 + k, col)

    def ring(v):
        return lax.rem(v + RING, RING)

    partner = (chip_row * 2 + 1 - k, col)

    def send(src, dst, group, r_sem, device):
        pltpu.make_async_remote_copy(
            src_ref=src, dst_ref=dst, send_sem=sent.at[group], recv_sem=r_sem, device_id=device, device_id_type=MESH
        ).start()

    def waiter(ref, group, r_sem):
        return pltpu.make_async_remote_copy(
            src_ref=ref, dst_ref=ref, send_sem=sent.at[group], recv_sem=r_sem, device_id=partner, device_id_type=MESH
        )

    def arrived(dst, r_sem):
        waiter(dst, 0, r_sem).wait_recv()

    def rows_of(xx, jj):
        zz = lax.rem(zh - jj + NZ, NZ)
        r = (lax.rem(xx + NX, NX) * NZ + zz) * 2 + k
        return pl.ds(pl.multiple_of(r * SLAB, SLAB), SLAB)

    my_rows = rows_of(x, 0)
    mine = xb.at[big * RING + small]
    own_w = [
        pltpu.make_async_copy(win_ref.at[zh], wb.at[pl.ds(0, 2), my_rows], local_sem.at[1]),
        pltpu.make_async_copy(wout_ref.at[zh], wb.at[2, my_rows], local_sem.at[2]),
    ]
    blocks = [
        pltpu.make_async_copy(src, dst, local_sem.at[3 + i])
        for i, (src, dst) in enumerate((
            (h_hbm, h_ref), (gain_hbm, gain_ref), (router_hbm, router_ref), (down_hbm, down_ref),
            (lengths_hbm, lengths), (ids_hbm, adapter_ids), (routes_hbm, routes_ref), (up_hbm, up_ref),
        ))
    ]
    own_x = pltpu.make_async_copy(h_hbm, mine, local_sem.at[0])
    for copy in own_w + blocks + [own_x]:
        copy.start()

    peers = [at_plane(ring(big + d), small) for d in range(1, RING)]
    peers += [at_plane(big, ring(small + d)) for d in range(1, RING)]
    peers += [at_x(x + d) for d in range(1, NX)] + [partner]
    barrier = pltpu.get_barrier_semaphore()
    for peer in peers:
        pl.semaphore_signal(barrier, inc=1, device_id=peer, device_id_type=MESH)
    pl.semaphore_wait(barrier, len(peers))

    offsets = (0, 1, -1, 2, -2, 3, -3, 4)

    def a_block(b, offset):
        return xb.at[ring(b) * RING + ring(small - offset)]

    def a_long_send(i, start, way, to_distance):
        b = big - start if way == 0 else big + start
        ahead = to_distance - start
        to = at_plane(ring(big + ahead), small) if way == 0 else at_plane(ring(big - ahead), small)
        dst = a_block(b, offsets[i])
        src = h_hbm if i == 0 and start == 0 else dst
        send(src, dst, 1, ab_r.at[way, i, to_distance - 1], to)

    def onward(two, i, way, d):
        last = 4 if i % 2 == way else 3
        if two:
            served = {0: (1, 2), 2: (3, 4)}.get(d, ())
        else:
            served = (d + 1,)
        return [v for v in served if v <= last]

    def a_long(i, d, way):
        b = big - d if way == 0 else big + d
        if d:
            arrived(a_block(b, offsets[i]), ab_r.at[way, i, d - 1])
        for v in onward(i in A_TWO, i, way, d):
            a_long_send(i, d, way, v)

    def a_short(i):
        arrived(a_block(big, offsets[i]), az_r.at[i])
        for w in range(2):
            a_long(i, 0, w)

    for i in range(1, RING):
        send(h_hbm, mine, 0, az_r.at[i], at_plane(big, ring(small + offsets[i])))
    for w in range(2):
        a_long(0, 0, w)

    for j in (1, 3, 2):
        e = lax.rem(zh + j, NZ)
        to = ((x * NZ + e) * 2 + k, col)
        send(win_ref.at[e], wb.at[pl.ds(0, 2), my_rows], 2, wz_r.at[j], to)
        send(wout_ref.at[e], wb.at[2, my_rows], 2, wz_r.at[j], to)

    def w_piece(xx, j):
        return wb.at[:, rows_of(xx, j)]

    def w_out(xx, j, slot, right=False, left=False, far=False):
        piece = w_piece(xx, j)
        if right:
            m = j if slot == 0 else 4 + j
            send(piece, piece, 3, wx_r.at[0, m], at_x(x + 1))
        if left:
            m = j if slot == 0 else 4 + j
            send(piece, piece, 3, wx_r.at[1, m], at_x(x - 1))
        if far:
            side = 0 if j < 2 else 1
            send(piece, piece, 3, wx_r.at[side, 4 + j], at_x(x + 2))
        send(piece, piece, 4, wp_r.at[slot // 3], partner)

    def w_own(j):
        if j == 0:
            for copy in own_w:
                copy.wait()
        else:
            arrived(w_piece(x, j), wz_r.at[j])
        w_out(x, j, 0, right=True, left=True, far=j in FAR)

    def w_near(j, way):
        if way == 0:
            arrived(w_piece(x - 1, j), wx_r.at[0, j])
            w_out(x - 1, j, 1, right=j < 2 and j not in FAR)
        else:
            arrived(w_piece(x + 1, j), wx_r.at[1, j])
            w_out(x + 1, j, 2, left=j >= 2 and j not in FAR)

    def w_far(j):
        side = 0 if j < 2 else 1
        arrived(w_piece(x + 2, j), wx_r.at[side, 4 + j])
        w_out(x + 2, j, 3)

    w_own(0)

    for copy in blocks:
        copy.wait()
    hx = h_ref[...].astype(F32)
    ones = jnp.ones((8, B), F32)
    squares = lax.dot_general(ones, hx * hx, NT, precision=HIGH, preferred_element_type=F32)
    scaled = hx * gain_ref[...]
    projected = lax.dot_general(down_ref[...].astype(F32), scaled, NT, precision=HIGH, preferred_element_type=F32)
    routed = lax.dot_general(router_ref[...].astype(F32), scaled, NT, precision=HIGH, preferred_element_type=F32)
    line = lax.broadcasted_iota(jnp.int32, (8, B), 0)
    tile = squares
    for e in range(NZ):
        tile = jnp.where(line == 1 + e, jnp.broadcast_to(routed[e : e + 1], (8, B)), tile)
    tile = jnp.where(line >= 5, 0.0, tile)
    tile = jnp.where(line == 5 + zl, jnp.broadcast_to(gain_ref[...], (8, B)), tile)
    position = row * B + lax.broadcasted_iota(jnp.int32, (1, B), 1)
    bound = lengths[0]
    request = (position >= bound).astype(jnp.int32)
    for i in range(1, REQUESTS):
        bound = bound + lengths[i]
        request = request + (position >= bound).astype(jnp.int32)
    adapter = jnp.zeros((1, B), jnp.int32)
    for i in range(REQUESTS):
        adapter = jnp.where(request == i, adapter_ids[i], adapter)
    adapter = jnp.broadcast_to(adapter, (RANK, B))
    part = jnp.zeros((RANK, B), F32)
    for a in range(ADAPTERS):
        part = part + jnp.where(adapter == a, projected[a * RANK : (a + 1) * RANK], 0.0)
    pstage[0, 0:8] = tile
    pstage[0, 8:24] = part
    other = (row, y * 2 + 1 - zl)
    send(pstage.at[0], pz, 6, pz_r.at[0], other)

    def pair_event():
        arrived(pz, pz_r.at[0])
        both = pz[...] + jnp.concatenate([tile, part], axis=0)
        pstage[1] = both
        pr[y] = both
        for d in range(1, RING):
            send(pstage.at[1], pr.at[y], 5, p_r.at[0], (row, ring(y + d) * 2 + zl))

    def gates_event():
        arrived(pr.at[pl.ds(0, RING - 1)], p_r.at[0])
        total = pr[0]
        for i in range(1, RING):
            total = total + pr[i]
        inverse = lax.rsqrt(total[0:1] / D + epsilon)
        logits = [total[1 + e : 2 + e] * inverse for e in range(NZ)]
        route = [routes_ref[0:1, :], routes_ref[1:2, :]]
        chosen = []
        for i in range(2):
            value = jnp.zeros((1, B), F32)
            for e in range(NZ):
                value = jnp.where(route[i] == e, logits[e], value)
            chosen.append(value)
        gates = [jax.nn.sigmoid(chosen[0] - chosen[1]), jax.nn.sigmoid(chosen[1] - chosen[0])]
        share = jnp.where(line == 0, jnp.broadcast_to(inverse, (8, B)), 0.0)
        for e in range(NZ):
            weight = jnp.where(route[0] == e, gates[0], 0.0) + jnp.where(route[1] == e, gates[1], 0.0)
            share = jnp.where(line == 1 + e, jnp.broadcast_to(weight, (8, B)), share)
        tr[zh] = share
        for d in range(1, NZ):
            to = ((x * NZ + lax.rem(zh + d, NZ)) * 2 + k, col)
            send(tr.at[zh], tr.at[zh], 7, t_r.at[0], to)
        return inverse, total[8:24] * jnp.broadcast_to(inverse, (RANK, B))

    def columns_event():
        arrived(tr.at[pl.ds(0, NZ - 1)], t_r.at[0])
        for i in range(NZ):
            rows = tr[i]
            gate_row = tr[i, pl.ds(1 + zh, 1), :]
            both = jnp.where(line == 0, rows, jnp.broadcast_to(gate_row, (8, B)))
            turned = jnp.transpose(both)
            inv_b[i] = jnp.broadcast_to(turned[:, 0:1], (B, B))
            gate_b[i] = jnp.broadcast_to(turned[:, 1:2], (B, B))

    events = [(P_AT[0], pair_event, ()), (P_AT[1], gates_event, ()), (P_AT[2], columns_event, ())]
    for i in range(RING):
        ready = A_READY[i]
        if i:
            events.append((ready, a_short, (i,)))
        for way in range(2):
            for d in range(1, 5 if i % 2 == way else 4):
                hops = ((d + 1) // 2 if i in A_TWO else d)
                events.append((ready + A_HOP * hops, a_long, (i, d, way)))
    for j, ready in enumerate(W_READY):
        for way in range(2):
            events.append((ready + W_AFTER[0], w_near, (j, way)))
        if j:
            events.append((ready, w_own, (j,)))
        events.append((ready + (W_AFTER[1] if j in FAR else W_AFTER[2]), w_far, (j,)))
    kept = {}
    for _, action, given in sorted(events, key=lambda event: event[0]):
        kept[action] = action(*given)
    latent = kept[gates_event][1]
    own_x.wait()

    @pl.loop(0, RING * RING)
    def _(i):
        yy, zz = lax.div(i, RING), lax.rem(i, RING)
        c, t = yy * 2 + lax.rem(zz, 2), lax.div(zz, 2)
        value = xb[yy * sy + zz * sz].astype(F32) * inv_b[t] * pr[yy, pl.ds(5 + lax.rem(zz, 2), 1), :]
        nb[pl.ds(pl.multiple_of(t * B, B), B), pl.ds(pl.multiple_of(c * B, B), B)] = value.astype(BF16)

    def contract(step, xx):
        part = pl.ds(pl.multiple_of(lax.rem(xx + NX, NX) * 512, 512), 512)

        @pl.loop(0, 1)
        def _(i):
            rows = pl.ds(pl.multiple_of(i * 512, 512), 512)
            tokens = nb[rows, part]
            sums = [jnp.dot(tokens, wb[n, part, :], preferred_element_type=F32) for n in range(2)]
            if step:
                sums = [acc[n, rows, :] + sums[n] for n in range(2)]
            if step < 3:
                for n in range(2):
                    acc[n, rows, :] = sums[n]
            else:
                hid[rows, :] = (jax.nn.silu(sums[0]) * sums[1]).astype(BF16)

    arrived(wb.at[:, pl.ds(0, 12 * SLAB)], wp_r.at[0])
    for step in range(3):
        contract(step, (x, x - 1, x + 1)[step])
    arrived(wb.at[:, pl.ds(0, 4 * SLAB)], wp_r.at[1])
    contract(3, x + 2)

    @pl.loop(0, RING)
    def _(yy):
        weights = wb[2, pl.ds(pl.multiple_of(yy * 256, 256), 256), :]
        result = lax.dot_general(hid[...], weights, NT, preferred_element_type=F32)
        for t in range(NZ):
            for half in range(2):
                block = result[t * B : (t + 1) * B, half * B : (half + 1) * B]
                ob[yy * sy + (t * 2 + half) * sz] = block * gate_b[t]

    targets = (4, 3, -3, 2, -2, 1, -1, 0)

    def r_sum(i, j, way, value):
        arrived(rs_recv.at[(way * RING + i) * 4 + j - 1], rs_r.at[way, i, j - 1])
        return value + rs_recv[(way * RING + i) * 4 + j - 1].astype(F32)

    def r_send(i, j, way):
        b = ring(big + j) if way == 0 else ring(big - j)
        value = ob[b * RING + ring(small + targets[i])]
        last = 4 if i % 2 == way else 3
        if i in O_TWO:
            sources = [v for v in (3, 4) if v <= last] if j == 2 else []
            ahead = {1: 1, 2: 2, 3: 1, 4: 2}[j]
        else:
            sources = [j + 1] if j < last else []
            ahead = 1
        for v in sources:
            value = r_sum(i, v, way, value)
        rs_send[(way * RING + i) * 4 + j - 1] = value.astype(BF16)
        to = at_plane(ring(big + ahead), small) if way == 0 else at_plane(ring(big - ahead), small)
        send(rs_send.at[(way * RING + i) * 4 + j - 1], rs_recv.at[(way * RING + i) * 4 + j - 1], 8, rs_r.at[way, i, j - 1], to)

    def r_last(i):
        s = ring(small + targets[i])
        value = ob[big * RING + s]
        for way in range(2):
            for v in (1, 2) if i in O_TWO else (1,):
                value = r_sum(i, v, way, value)
        if targets[i]:
            sm_send[i] = value.astype(BF16)
            send(sm_send.at[i], sm_recv.at[i], 9, sm_r.at[0], at_plane(big, s))
        return value

    def delta_event():
        spread = jnp.concatenate([jnp.where(adapter == a, latent, 0.0) for a in range(ADAPTERS)], axis=0)
        delta = lax.dot_general(spread, up_ref[...].astype(F32), TN, precision=HIGH, preferred_element_type=F32)
        return delta

    events = [(7.0, delta_event, ())]
    for i in range(RING):
        for way in range(2):
            first = 4 if i % 2 == way else 3
            for j in range(1, first + 1):
                when = (O_TWO_AT if i in O_TWO else O_RING_AT)[first == 3][j - 1] + O_SPREAD * i
                events.append((when, r_send, (i, j, way)))
        events.append((O_LAST_AT[i in O_TWO] + O_SPREAD * i, r_last, (i,)))
    for _, action, given in sorted(events, key=lambda event: event[0]):
        kept[action] = action(*given)
    result = kept[r_last] + adapter_scaling_factor * kept[delta_event]
    arrived(sm_recv.at[pl.ds(0, RING - 1)], sm_r.at[0])
    for i in range(RING - 1):
        result = result + sm_recv[i].astype(F32)
    out_ref[...] = result.astype(BF16)
    for group, ref in enumerate((
        xb.at[pl.ds(0, 7)], xb.at[pl.ds(0, 56)], wb.at[:, pl.ds(0, 3 * SLAB)], wb.at[:, pl.ds(0, 12 * SLAB)],
        wb.at[:, pl.ds(0, 16 * SLAB)], pr.at[pl.ds(0, 7)], pz, tr.at[pl.ds(0, 3)],
        rs_send.at[pl.ds(0, 56)], sm_send.at[pl.ds(0, 7)],
    )):
        waiter(ref, group, pz_r.at[0]).wait_send()


def on_device(
    hidden_input, norm_gain, router_weight, expert_in, expert_out, adapter_down, adapter_up, routes, lengths, adapter_ids
):
    down = jnp.transpose(adapter_down, (0, 2, 1)).reshape(ADAPTERS * RANK, B)
    vmem = pl.BlockSpec(memory_space=pltpu.VMEM)
    hbm = pl.BlockSpec(memory_space=pltpu.HBM)
    dma = pltpu.SemaphoreType.DMA
    return pl.pallas_call(
        kernel,
        out_shape=jax.ShapeDtypeStruct((B, B), BF16),
        in_specs=[hbm] * 10,
        out_specs=vmem,
        scratch_shapes=[
            pltpu.SMEM((REQUESTS,), jnp.int32),
            pltpu.SMEM((REQUESTS,), jnp.int32),
            pltpu.VMEM((B, B), BF16),
            pltpu.VMEM((1, B), F32),
            pltpu.VMEM((NZ, B), BF16),
            pltpu.VMEM((ADAPTERS * RANK, B), BF16),
            pltpu.VMEM((ADAPTERS * RANK, B), BF16),
            pltpu.VMEM((2, B), jnp.int32),
            pltpu.VMEM((RING * RING, B, B), BF16),
            pltpu.VMEM((NZ * B, D), BF16),
            pltpu.VMEM((3, D, F), BF16),
            pltpu.VMEM((RING * RING, B, B), F32),
            pltpu.VMEM((NZ * B, F), BF16),
            pltpu.VMEM((RING, 24, B), F32),
            pltpu.VMEM((24, B), F32),
            pltpu.VMEM((NZ, 8, B), F32),
            pltpu.VMEM((NZ, B, B), F32),
            pltpu.VMEM((NZ, B, B), F32),
            pltpu.VMEM((2, 24, B), F32),
            pltpu.VMEM((8 * RING, B, B), BF16),
            pltpu.VMEM((8 * RING, B, B), BF16),
            pltpu.VMEM((RING, B, B), BF16),
            pltpu.VMEM((RING, B, B), BF16),
            pltpu.VMEM((2, NZ * B, F), F32),
            dma((11,)),
            dma((10,)),
            dma((RING,)),
            dma((2, RING, 4)),
            dma((NZ,)),
            dma((2, 8)),
            dma((2,)),
            dma((1,)), dma((1,)), dma((1,)),
            dma((2, RING, 4)),
            dma((1,)),
        ],
        compiler_params=pltpu.CompilerParams(
            collective_id=0, has_side_effects=True
        ),
    )(
        lengths, adapter_ids, hidden_input, norm_gain[None, :], router_weight.T, down,
        adapter_up.reshape(ADAPTERS * RANK, B), routes.T, expert_in, jnp.transpose(expert_out, (0, 2, 1)),
    )


def solution(mesh):
    placed = (
        P("row", "col"),
        P("col"),
        P("col", None),
        P(None, None, "row", "col"),
        P(None, "col", "row"),
        P(None, "col", None),
        P(None, None, "col"),
        P("row", None),
        P(),
        P(),
    )
    return jax.shard_map(
        on_device, mesh=mesh, in_specs=placed, out_specs=P("row", "col"), check_vma=False
    )
```

```python
import jax
import jax.numpy as jnp
from jax import lax
from jax.experimental import pallas as pl
from jax.experimental.pallas import tpu as pltpu
from jax.sharding import PartitionSpec as P

NX, NZ, NC = 4, 4, 16
RING = 8
B = 128
D = 2048
F = 256
SLAB = 64
RANK, ADAPTERS, REQUESTS = 16, 16, 16
A_TWO = (5, 6, 7)
O_TWO = (0, 1, 2)
FAR = (2,)
A_READY = (0.0, 5.0, 5.1, 6.0, 6.1, 7.0, 7.1, 8.5)
W_READY = (0.0, 8.5, 14.0, 9.0)
O_RING_AT = ((11.1, 7.4, 3.7, -2.0), (7.4, 3.7, -2.0))
O_TWO_AT = ((8.3, 5.8, 0.7, 0.5), (8.3, 5.8, 0.6))
O_LAST_AT = (15.0, 13.2)
O_SPREAD = 0.1
P_AT = (9.0, 17.0, 26.0)
A_HOP = 3.9
W_AFTER = (4.0, 5.0, 8.0)
epsilon = 1e-05
adapter_scaling_factor = 2.0

MESH = pl.DeviceIdType.MESH
F32, BF16 = jnp.float32, jnp.bfloat16
HIGH = lax.Precision.HIGHEST
NT = (((1,), (1,)), ((), ()))
TN = (((0,), (0,)), ((), ()))


def kernel(
    lengths_hbm, ids_hbm, h_hbm, gain_hbm, router_hbm, down_hbm, up_hbm, routes_hbm, win_ref, wout_ref, out_ref,
    lengths, adapter_ids, h_ref, gain_ref, router_ref, down_ref, up_ref, routes_ref,
    xb, nb, wb, ob, hid, pr, pz, tr, inv_b, gate_b, pstage,
    rs_send, rs_recv, sm_send, sm_recv,
    acc, local_sem, sent, az_r, ab_r, wz_r, wx_r, wp_r, p_r, pz_r, t_r, rs_r, sm_r,
):
    row, col = lax.axis_index("row"), lax.axis_index("col")
    k = lax.rem(row, 2)
    chip_row = lax.div(row, 2)
    x, zh = lax.div(chip_row, NZ), lax.rem(chip_row, NZ)
    y, zl = lax.div(col, 2), lax.rem(col, 2)
    z = zh * 2 + zl
    big, small = y * (1 - k) + z * k, z * (1 - k) + y * k
    sy, sz = RING * (1 - k) + k, RING * k + (1 - k)

    def at_plane(b, s):
        yy, zz = b * (1 - k) + s * k, s * (1 - k) + b * k
        return ((x * NZ + lax.div(zz, 2)) * 2 + k, yy * 2 + lax.rem(zz, 2))

    def at_x(xx):
        return ((lax.rem(xx + NX, NX) * NZ + zh) * 2 + k, col)

    def ring(v):
        return lax.rem(v + RING, RING)

    partner = (chip_row * 2 + 1 - k, col)

    def send(src, dst, group, r_sem, device):
        pltpu.make_async_remote_copy(
            src_ref=src, dst_ref=dst, send_sem=sent.at[group], recv_sem=r_sem, device_id=device, device_id_type=MESH
        ).start()

    def waiter(ref, group, r_sem):
        return pltpu.make_async_remote_copy(
            src_ref=ref, dst_ref=ref, send_sem=sent.at[group], recv_sem=r_sem, device_id=partner, device_id_type=MESH
        )

    def arrived(dst, r_sem):
        waiter(dst, 0, r_sem).wait_recv()

    def rows_of(xx, jj):
        zz = lax.rem(zh - jj + NZ, NZ)
        r = (lax.rem(xx + NX, NX) * NZ + zz) * 2 + k
        return pl.ds(pl.multiple_of(r * SLAB, SLAB), SLAB)

    my_rows = rows_of(x, 0)
    mine = xb.at[big * RING + small]
    own_w = [
        pltpu.make_async_copy(win_ref.at[zh], wb.at[pl.ds(0, 2), my_rows], local_sem.at[1]),
        pltpu.make_async_copy(wout_ref.at[zh], wb.at[2, my_rows], local_sem.at[2]),
    ]
    blocks = [
        pltpu.make_async_copy(src, dst, local_sem.at[3 + i])
        for i, (src, dst) in enumerate((
            (h_hbm, h_ref), (gain_hbm, gain_ref), (router_hbm, router_ref), (down_hbm, down_ref),
            (lengths_hbm, lengths), (ids_hbm, adapter_ids), (routes_hbm, routes_ref), (up_hbm, up_ref),
        ))
    ]
    own_x = pltpu.make_async_copy(h_hbm, mine, local_sem.at[0])
    for copy in own_w + blocks + [own_x]:
        copy.start()

    peers = [at_plane(ring(big + d), small) for d in range(1, RING)]
    peers += [at_plane(big, ring(small + d)) for d in range(1, RING)]
    peers += [at_x(x + d) for d in range(1, NX)] + [partner]
    barrier = pltpu.get_barrier_semaphore()
    for peer in peers:
        pl.semaphore_signal(barrier, inc=1, device_id=peer, device_id_type=MESH)
    pl.semaphore_wait(barrier, len(peers))

    offsets = (0, 1, -1, 2, -2, 3, -3, 4)

    def a_block(b, offset):
        return xb.at[ring(b) * RING + ring(small - offset)]

    def a_long_send(i, start, way, to_distance):
        b = big - start if way == 0 else big + start
        ahead = to_distance - start
        to = at_plane(ring(big + ahead), small) if way == 0 else at_plane(ring(big - ahead), small)
        dst = a_block(b, offsets[i])
        src = h_hbm if i == 0 and start == 0 else dst
        send(src, dst, 1, ab_r.at[way, i, to_distance - 1], to)

    def onward(two, i, way, d):
        last = 4 if i % 2 == way else 3
        if two:
            served = {0: (1, 2), 2: (3, 4)}.get(d, ())
        else:
            served = (d + 1,)
        return [v for v in served if v <= last]

    def a_long(i, d, way):
        b = big - d if way == 0 else big + d
        if d:
            arrived(a_block(b, offsets[i]), ab_r.at[way, i, d - 1])
        for v in onward(i in A_TWO, i, way, d):
            a_long_send(i, d, way, v)

    def a_short(i):
        arrived(a_block(big, offsets[i]), az_r.at[i])
        for w in range(2):
            a_long(i, 0, w)

    for i in range(1, RING):
        send(h_hbm, mine, 0, az_r.at[i], at_plane(big, ring(small + offsets[i])))
    for w in range(2):
        a_long(0, 0, w)

    for j in (1, 3, 2):
        e = lax.rem(zh + j, NZ)
        to = ((x * NZ + e) * 2 + k, col)
        send(win_ref.at[e], wb.at[pl.ds(0, 2), my_rows], 2, wz_r.at[j], to)
        send(wout_ref.at[e], wb.at[2, my_rows], 2, wz_r.at[j], to)

    def w_piece(xx, j):
        return wb.at[:, rows_of(xx, j)]

    def w_out(xx, j, slot, right=False, left=False, far=False):
        piece = w_piece(xx, j)
        if right:
            m = j if slot == 0 else 4 + j
            send(piece, piece, 3, wx_r.at[0, m], at_x(x + 1))
        if left:
            m = j if slot == 0 else 4 + j
            send(piece, piece, 3, wx_r.at[1, m], at_x(x - 1))
        if far:
            side = 0 if j < 2 else 1
            send(piece, piece, 3, wx_r.at[side, 4 + j], at_x(x + 2))
        send(piece, piece, 4, wp_r.at[slot // 3], partner)

    def w_own(j):
        if j == 0:
            for copy in own_w:
                copy.wait()
        else:
            arrived(w_piece(x, j), wz_r.at[j])
        w_out(x, j, 0, right=True, left=True, far=j in FAR)

    def w_near(j, way):
        if way == 0:
            arrived(w_piece(x - 1, j), wx_r.at[0, j])
            w_out(x - 1, j, 1, right=j < 2 and j not in FAR)
        else:
            arrived(w_piece(x + 1, j), wx_r.at[1, j])
            w_out(x + 1, j, 2, left=j >= 2 and j not in FAR)

    def w_far(j):
        side = 0 if j < 2 else 1
        arrived(w_piece(x + 2, j), wx_r.at[side, 4 + j])
        w_out(x + 2, j, 3)

    w_own(0)

    for copy in blocks:
        copy.wait()
    hx = h_ref[...].astype(F32)
    ones = jnp.ones((8, B), F32)
    squares = lax.dot_general(ones, hx * hx, NT, precision=HIGH, preferred_element_type=F32)
    scaled = hx * gain_ref[...]
    projected = lax.dot_general(down_ref[...].astype(F32), scaled, NT, precision=HIGH, preferred_element_type=F32)
    routed = lax.dot_general(router_ref[...].astype(F32), scaled, NT, precision=HIGH, preferred_element_type=F32)
    line = lax.broadcasted_iota(jnp.int32, (8, B), 0)
    tile = squares
    for e in range(NZ):
        tile = jnp.where(line == 1 + e, jnp.broadcast_to(routed[e : e + 1], (8, B)), tile)
    tile = jnp.where(line >= 5, 0.0, tile)
    tile = jnp.where(line == 5 + zl, jnp.broadcast_to(gain_ref[...], (8, B)), tile)
    position = row * B + lax.broadcasted_iota(jnp.int32, (1, B), 1)
    bound = lengths[0]
    request = (position >= bound).astype(jnp.int32)
    for i in range(1, REQUESTS):
        bound = bound + lengths[i]
        request = request + (position >= bound).astype(jnp.int32)
    adapter = jnp.zeros((1, B), jnp.int32)
    for i in range(REQUESTS):
        adapter = jnp.where(request == i, adapter_ids[i], adapter)
    adapter = jnp.broadcast_to(adapter, (RANK, B))
    part = jnp.zeros((RANK, B), F32)
    for a in range(ADAPTERS):
        part = part + jnp.where(adapter == a, projected[a * RANK : (a + 1) * RANK], 0.0)
    pstage[0, 0:8] = tile
    pstage[0, 8:24] = part
    other = (row, y * 2 + 1 - zl)
    send(pstage.at[0], pz, 6, pz_r.at[0], other)

    def pair_event():
        arrived(pz, pz_r.at[0])
        both = pz[...] + jnp.concatenate([tile, part], axis=0)
        pstage[1] = both
        pr[y] = both
        for d in range(1, RING):
            send(pstage.at[1], pr.at[y], 5, p_r.at[0], (row, ring(y + d) * 2 + zl))

    def gates_event():
        arrived(pr.at[pl.ds(0, RING - 1)], p_r.at[0])
        total = pr[0]
        for i in range(1, RING):
            total = total + pr[i]
        inverse = lax.rsqrt(total[0:1] / D + epsilon)
        logits = [total[1 + e : 2 + e] * inverse for e in range(NZ)]
        route = [routes_ref[0:1, :], routes_ref[1:2, :]]
        chosen = []
        for i in range(2):
            value = jnp.zeros((1, B), F32)
            for e in range(NZ):
                value = jnp.where(route[i] == e, logits[e], value)
            chosen.append(value)
        gates = [jax.nn.sigmoid(chosen[0] - chosen[1]), jax.nn.sigmoid(chosen[1] - chosen[0])]
        share = jnp.where(line == 0, jnp.broadcast_to(inverse, (8, B)), 0.0)
        for e in range(NZ):
            weight = jnp.where(route[0] == e, gates[0], 0.0) + jnp.where(route[1] == e, gates[1], 0.0)
            share = jnp.where(line == 1 + e, jnp.broadcast_to(weight, (8, B)), share)
        tr[zh] = share
        for d in range(1, NZ):
            to = ((x * NZ + lax.rem(zh + d, NZ)) * 2 + k, col)
            send(tr.at[zh], tr.at[zh], 7, t_r.at[0], to)
        return inverse, total[8:24] * jnp.broadcast_to(inverse, (RANK, B))

    def columns_event():
        arrived(tr.at[pl.ds(0, NZ - 1)], t_r.at[0])
        for i in range(NZ):
            rows = tr[i]
            gate_row = tr[i, pl.ds(1 + zh, 1), :]
            both = jnp.where(line == 0, rows, jnp.broadcast_to(gate_row, (8, B)))
            turned = jnp.transpose(both)
            inv_b[i] = jnp.broadcast_to(turned[:, 0:1], (B, B))
            gate_b[i] = jnp.broadcast_to(turned[:, 1:2], (B, B))

    events = [(P_AT[0], pair_event, ()), (P_AT[1], gates_event, ()), (P_AT[2], columns_event, ())]
    for i in range(RING):
        ready = A_READY[i]
        if i:
            events.append((ready, a_short, (i,)))
        for way in range(2):
            for d in range(1, 5 if i % 2 == way else 4):
                hops = ((d + 1) // 2 if i in A_TWO else d)
                events.append((ready + A_HOP * hops, a_long, (i, d, way)))
    for j, ready in enumerate(W_READY):
        for way in range(2):
            events.append((ready + W_AFTER[0], w_near, (j, way)))
        if j:
            events.append((ready, w_own, (j,)))
        events.append((ready + (W_AFTER[1] if j in FAR else W_AFTER[2]), w_far, (j,)))
    kept = {}
    for _, action, given in sorted(events, key=lambda event: event[0]):
        kept[action] = action(*given)
    latent = kept[gates_event][1]
    own_x.wait()

    @pl.loop(0, RING * RING)
    def _(i):
        yy, zz = lax.div(i, RING), lax.rem(i, RING)
        c, t = yy * 2 + lax.rem(zz, 2), lax.div(zz, 2)
        value = xb[yy * sy + zz * sz].astype(F32) * inv_b[t] * pr[yy, pl.ds(5 + lax.rem(zz, 2), 1), :]
        nb[pl.ds(pl.multiple_of(t * B, B), B), pl.ds(pl.multiple_of(c * B, B), B)] = value.astype(BF16)

    arrived(wb.at[:, pl.ds(0, 12 * SLAB)], wp_r.at[0])
    arrived(wb.at[:, pl.ds(0, 4 * SLAB)], wp_r.at[1])
    gate = jnp.dot(nb[...], wb[0], preferred_element_type=F32)
    up = jnp.dot(nb[...], wb[1], preferred_element_type=F32)
    hid[...] = (jax.nn.silu(gate) * up).astype(BF16)

    @pl.loop(0, RING)
    def _(yy):
        weights = wb[2, pl.ds(pl.multiple_of(yy * 256, 256), 256), :]
        result = lax.dot_general(hid[...], weights, NT, preferred_element_type=F32)
        for t in range(NZ):
            for half in range(2):
                block = result[t * B : (t + 1) * B, half * B : (half + 1) * B]
                ob[yy * sy + (t * 2 + half) * sz] = block * gate_b[t]

    targets = (4, 3, -3, 2, -2, 1, -1, 0)

    def r_sum(i, j, way, value):
        arrived(rs_recv.at[(way * RING + i) * 4 + j - 1], rs_r.at[way, i, j - 1])
        return value + rs_recv[(way * RING + i) * 4 + j - 1].astype(F32)

    def r_send(i, j, way):
        b = ring(big + j) if way == 0 else ring(big - j)
        value = ob[b * RING + ring(small + targets[i])]
        last = 4 if i % 2 == way else 3
        if i in O_TWO:
            sources = [v for v in (3, 4) if v <= last] if j == 2 else []
            ahead = {1: 1, 2: 2, 3: 1, 4: 2}[j]
        else:
            sources = [j + 1] if j < last else []
            ahead = 1
        for v in sources:
            value = r_sum(i, v, way, value)
        rs_send[(way * RING + i) * 4 + j - 1] = value.astype(BF16)
        to = at_plane(ring(big + ahead), small) if way == 0 else at_plane(ring(big - ahead), small)
        send(rs_send.at[(way * RING + i) * 4 + j - 1], rs_recv.at[(way * RING + i) * 4 + j - 1], 8, rs_r.at[way, i, j - 1], to)

    def r_last(i):
        s = ring(small + targets[i])
        value = ob[big * RING + s]
        for way in range(2):
            for v in (1, 2) if i in O_TWO else (1,):
                value = r_sum(i, v, way, value)
        if targets[i]:
            sm_send[i] = value.astype(BF16)
            send(sm_send.at[i], sm_recv.at[i], 9, sm_r.at[0], at_plane(big, s))
        return value

    def delta_event():
        spread = jnp.concatenate([jnp.where(adapter == a, latent, 0.0) for a in range(ADAPTERS)], axis=0)
        delta = lax.dot_general(spread, up_ref[...].astype(F32), TN, precision=HIGH, preferred_element_type=F32)
        return delta

    events = [(7.0, delta_event, ())]
    for i in range(RING):
        for way in range(2):
            first = 4 if i % 2 == way else 3
            for j in range(1, first + 1):
                when = (O_TWO_AT if i in O_TWO else O_RING_AT)[first == 3][j - 1] + O_SPREAD * i
                events.append((when, r_send, (i, j, way)))
        events.append((O_LAST_AT[i in O_TWO] + O_SPREAD * i, r_last, (i,)))
    for _, action, given in sorted(events, key=lambda event: event[0]):
        kept[action] = action(*given)
    result = kept[r_last] + adapter_scaling_factor * kept[delta_event]
    arrived(sm_recv.at[pl.ds(0, RING - 1)], sm_r.at[0])
    for i in range(RING - 1):
        result = result + sm_recv[i].astype(F32)
    out_ref[...] = result.astype(BF16)
    for group, ref in enumerate((
        xb.at[pl.ds(0, 7)], xb.at[pl.ds(0, 56)], wb.at[:, pl.ds(0, 3 * SLAB)], wb.at[:, pl.ds(0, 12 * SLAB)],
        wb.at[:, pl.ds(0, 16 * SLAB)], pr.at[pl.ds(0, 7)], pz, tr.at[pl.ds(0, 3)],
        rs_send.at[pl.ds(0, 56)], sm_send.at[pl.ds(0, 7)],
    )):
        waiter(ref, group, pz_r.at[0]).wait_send()


def on_device(
    hidden_input, norm_gain, router_weight, expert_in, expert_out, adapter_down, adapter_up, routes, lengths, adapter_ids
):
    down = jnp.transpose(adapter_down, (0, 2, 1)).reshape(ADAPTERS * RANK, B)
    vmem = pl.BlockSpec(memory_space=pltpu.VMEM)
    hbm = pl.BlockSpec(memory_space=pltpu.HBM)
    dma = pltpu.SemaphoreType.DMA
    return pl.pallas_call(
        kernel,
        out_shape=jax.ShapeDtypeStruct((B, B), BF16),
        in_specs=[hbm] * 10,
        out_specs=vmem,
        scratch_shapes=[
            pltpu.SMEM((REQUESTS,), jnp.int32),
            pltpu.SMEM((REQUESTS,), jnp.int32),
            pltpu.VMEM((B, B), BF16),
            pltpu.VMEM((1, B), F32),
            pltpu.VMEM((NZ, B), BF16),
            pltpu.VMEM((ADAPTERS * RANK, B), BF16),
            pltpu.VMEM((ADAPTERS * RANK, B), BF16),
            pltpu.VMEM((2, B), jnp.int32),
            pltpu.VMEM((RING * RING, B, B), BF16),
            pltpu.VMEM((NZ * B, D), BF16),
            pltpu.VMEM((3, D, F), BF16),
            pltpu.VMEM((RING * RING, B, B), F32),
            pltpu.VMEM((NZ * B, F), BF16),
            pltpu.VMEM((RING, 24, B), F32),
            pltpu.VMEM((24, B), F32),
            pltpu.VMEM((NZ, 8, B), F32),
            pltpu.VMEM((NZ, B, B), F32),
            pltpu.VMEM((NZ, B, B), F32),
            pltpu.VMEM((2, 24, B), F32),
            pltpu.VMEM((8 * RING, B, B), BF16),
            pltpu.VMEM((8 * RING, B, B), BF16),
            pltpu.VMEM((RING, B, B), BF16),
            pltpu.VMEM((RING, B, B), BF16),
            pltpu.VMEM((2, NZ * B, F), F32),
            dma((11,)),
            dma((10,)),
            dma((RING,)),
            dma((2, RING, 4)),
            dma((NZ,)),
            dma((2, 8)),
            dma((2,)),
            dma((1,)), dma((1,)), dma((1,)),
            dma((2, RING, 4)),
            dma((1,)),
        ],
        compiler_params=pltpu.CompilerParams(
            collective_id=0, has_side_effects=True
        ),
    )(
        lengths, adapter_ids, hidden_input, norm_gain[None, :], router_weight.T, down,
        adapter_up.reshape(ADAPTERS * RANK, B), routes.T, expert_in, jnp.transpose(expert_out, (0, 2, 1)),
    )


def solution(mesh):
    placed = (
        P("row", "col"),
        P("col"),
        P("col", None),
        P(None, None, "row", "col"),
        P(None, "col", "row"),
        P(None, "col", None),
        P(None, None, "col"),
        P("row", None),
        P(),
        P(),
    )
    return jax.shard_map(
        on_device, mesh=mesh, in_specs=placed, out_specs=P("row", "col"), check_vma=False
    )
```
